256 devices in a mesh: samp: 4 (over y_lo, core), snp: 64 (over x, z, y_hi).
Axes of the slice: x: 4, y: 4 (y_hi: 2, y_lo: 2; y = y_hi * 2 + y_lo), z: 8, core: 2. Of those that a mesh axis runs over, the one named last changes fastest.
Arguments:
- dosage: int32 [3072, 2048], P('snp', 'samp'), may hold values from 0 to 2
- pheno: bfloat16 [2048, 2048], P('samp'), may hold values from -6 to 6
- perm: int32 [8, 2048], P(None, 'samp'), may hold values from 0 to 2047, each once within a row
- snp_weight: float32 [3072], P('snp'), may hold values from 0.015 to 64
Outputs:
- whitened: bfloat16 [9, 3072, 2048], P(None, 'snp', 'samp')
The draws below stay inside these ranges and needn't reach their ends.
Inputs may be any that keep to these rules, and one draw needn't show every extreme that they name: `perm`: each of the 8 rows names every sample index exactly once.
All inputs are finite; a program needn't handle non-finite values.
Results may differ from the reference program's by a relative error of at most 0.012.
Values may be sent and summed in bfloat16 or wider, within the bound.
A program may use at most 64 MiB of HBM per device.

```python
import jax
import jax.numpy as jnp
from jax import lax

G = 2048
NULLS = 8
SNP_DEV = 48
COPIES = 9
NS = 2048
NSNP = 3072


def draw_snp_weight(key, part):
    slabs = NSNP // SNP_DEV
    slab_draw = jax.random.uniform(jax.random.fold_in(key, 11), (slabs,), jnp.float32)
    snp_draw = jax.random.uniform(jax.random.fold_in(key, 12), (NSNP,), jnp.float32)
    exponent = jnp.repeat(2.0 * slab_draw - 1.0, SNP_DEV) + 0.2 * (2.0 * snp_draw - 1.0)
    return jnp.power(10.0, exponent).astype(jnp.float32)


def draw_pheno(key, part):
    values = jax.random.normal(jax.random.fold_in(key, 24), (NS, G), jnp.float32)
    return jnp.clip(values, -6.0, 6.0).astype(jnp.bfloat16)


def place_ends(values, stream_key, low, largest):
    shape = values.shape
    index_at = [jax.random.randint(jax.random.fold_in(stream_key, axis), (), 0, shape[axis]) for axis in range(len(shape))]
    values = values.at[tuple(index_at)].set(low)
    longest = shape.index(max(shape))
    index_at[longest] = (index_at[longest] + 1) % shape[longest]
    return values.at[tuple(index_at)].set(largest)


def setup_inputs(seed: int = 0) -> dict:
    seeds = jax.random.split(jax.random.key(seed), 5)
    dosage = place_ends(jax.random.randint(seeds[0], (NSNP, NS), 0, 3), jax.random.fold_in(seeds[0], 1), 0, 2).astype(jnp.int32)
    pheno = draw_pheno(jax.random.fold_in(seeds[4], 71), 0)
    perm = jax.vmap(lambda own: jax.random.permutation(own, NS))(jax.random.split(seeds[2], NULLS)).reshape((NULLS, NS)).astype(jnp.int32)
    snp_weight = draw_snp_weight(jax.random.fold_in(seeds[4], 71), 0)
    return dict(dosage=dosage, pheno=pheno, perm=perm, snp_weight=snp_weight)


def reference(dosage, pheno, perm, snp_weight):
    dose = dosage.astype(jnp.float32)
    dose_mean = lax.optimization_barrier(jnp.mean(dose, axis=1))
    dose_square = lax.optimization_barrier(jnp.mean(dose * dose, axis=1))
    pheno_total = lax.optimization_barrier(jnp.sum(pheno.astype(jnp.float32), axis=0))
    dose_half = dosage.astype(jnp.bfloat16)
    own_rows = jnp.arange(NS).astype(jnp.int32)
    sources = jnp.concatenate([own_rows[None, :], perm.astype(jnp.int32)], axis=0)

    def one_copy(source):
        return jnp.dot(dose_half, pheno[source], preferred_element_type=jnp.float32)
    raw_scores = lax.map(one_copy, sources)
    spread = jnp.sqrt(NS * (dose_square + 1e-05))
    scores = ((raw_scores - dose_mean[None, :, None] * pheno_total[None, None, :]) / spread[None, :, None]).astype(jnp.bfloat16)
    flat = scores.reshape(COPIES * NSNP, G)
    null_scores = flat[NSNP:]
    weight_rows = jnp.tile(snp_weight.astype(jnp.float32), NULLS)[:, None]
    weighted = (null_scores.astype(jnp.float32) * weight_rows).astype(jnp.bfloat16)
    gram = lax.dot_general(weighted, null_scores, (((0,), (0,)), ((), ())), preferred_element_type=jnp.float32) / (NULLS * NSNP)
    scale = jnp.trace(gram) / G + 1e-06
    scaled = gram / scale
    identity = jnp.eye(G, dtype=jnp.float32)
    first_step = ((3.0 * identity - scaled) * 0.5).astype(jnp.bfloat16)
    first_image = jnp.dot(scaled.astype(jnp.bfloat16), first_step, preferred_element_type=jnp.float32).astype(jnp.bfloat16)
    second_prod = jnp.dot(first_step, first_image, preferred_element_type=jnp.float32)
    second_step = ((3.0 * identity - second_prod) * 0.5).astype(jnp.bfloat16)
    root_approx = jnp.dot(second_step, first_step, preferred_element_type=jnp.float32)
    root_matrix = (root_approx / jnp.sqrt(scale)).astype(jnp.bfloat16)
    white = jnp.dot(flat, root_matrix, preferred_element_type=jnp.float32)
    return white.astype(jnp.bfloat16).reshape(COPIES, NSNP, G)
```

```python
import jax
import jax.numpy as jnp
from jax import lax
from jax.sharding import Mesh
from jax.sharding import PartitionSpec as P

SAMP = ("y_lo", "core")
SNP = ("x", "z", "y_hi")
F32 = jnp.float32
BF16 = jnp.bfloat16
NT = (((1,), (1,)), ((), ()))
LOW = 256


def sent_parts(array, axis):
    return lax.all_to_all(array, axis, split_axis=0, concat_axis=0, tiled=True)


def copies_from(array, axis):
    devices = lax.axis_size(axis)
    return sent_parts(jnp.broadcast_to(array[None], (devices, *array.shape)), axis)


def summed_share(array, axis):
    devices = lax.axis_size(axis)
    rows = array.shape[0] // devices
    arrived = sent_parts(array.astype(BF16).reshape(devices, rows, array.shape[1]), axis)
    return jnp.sum(arrived.astype(F32), axis=0)


def gathered_rows(array, axis):
    got = copies_from(array, axis)
    return got.reshape(got.shape[0] * got.shape[1], got.shape[2])


def shards(dosage, pheno, perm, snp_weight):
    snps, own = dosage.shape
    genes = pheno.shape[1]
    groups = lax.axis_size(SAMP)
    samples = own * groups
    total_snps = snps * lax.axis_size(SNP)
    nulls = perm.shape[0]
    copies = nulls + 1
    rows = copies * snps
    cols = genes // groups
    me = lax.axis_index(SAMP)
    coded = jnp.concatenate(
        [dosage, perm // LOW, perm % LOW], axis=0
    ).astype(BF16)
    coded = copies_from(coded, SAMP)
    coded = jnp.moveaxis(coded, 0, 1).reshape(coded.shape[1], samples)
    pheno_parts = jnp.moveaxis(pheno.reshape(own, groups, cols), 1, 0)
    pheno_cols = sent_parts(pheno_parts, SAMP).reshape(samples, cols)
    dose = coded[:snps]
    high = coded[snps : snps + nulls]
    low = coded[snps + nulls :]
    steps = samples // LOW
    step_ids = jnp.arange(steps).astype(BF16)[:, None, None]
    low_ids = jnp.arange(LOW).astype(BF16)[:, None]
    placed = [dose]
    for k in range(nulls):
        masked = jnp.where(high[k][None, None, :] == step_ids, dose[None], jnp.zeros((), BF16))
        onehot = (low[k][None, :] == low_ids).astype(BF16)
        part = lax.dot_general(
            masked.reshape(steps * snps, samples), onehot, NT, preferred_element_type=F32
        ).astype(BF16)
        part = part.reshape(steps, snps, LOW)
        placed.append(jnp.concatenate([part[h] for h in range(steps)], axis=1))
    placed = jnp.concatenate(placed, axis=0)
    raw = jnp.dot(placed, pheno_cols, preferred_element_type=F32)
    dose32 = dose.astype(F32)
    dose_mean = jnp.sum(dose32, axis=1) / samples
    dose_square = jnp.sum(dose32 * dose32, axis=1) / samples
    pheno_sum = jnp.sum(pheno_cols.astype(F32), axis=0)
    spread = jnp.sqrt(samples * (dose_square + 1e-05))
    mean_rows = jnp.tile(dose_mean, copies)[:, None]
    spread_rows = jnp.tile(spread, copies)[:, None]
    scores = ((raw - mean_rows * pheno_sum[None, :]) / spread_rows).astype(BF16)
    every = copies_from(scores, SAMP)
    every = jnp.moveaxis(every, 0, 1).reshape(rows, genes)
    weight_rows = jnp.tile(snp_weight, nulls)[:, None]
    weighted = (every[snps:].astype(F32) * weight_rows).astype(BF16)
    gram = lax.dot_general(
        weighted, scores[snps:], (((0,), (0,)), ((), ())), preferred_element_type=F32
    )
    for axis in ("x", "y_hi", "z"):
        gram = summed_share(gram, axis)
    gram = (gram / (nulls * total_snps)).astype(BF16)
    for axis in ("z", "y_hi", "x"):
        gram = gathered_rows(gram, axis)
    gram = copies_from(gram, SAMP)
    trace_value = F32(0)
    for a in range(groups):
        block = gram[a, a * cols : (a + 1) * cols].astype(F32)
        trace_value += jnp.sum(jnp.where(jnp.eye(cols, dtype=bool), block, F32(0)))
    scale = trace_value / genes + 1e-06

    def image(left):
        left = left.astype(BF16)
        parts = [jnp.dot(left, gram[a], preferred_element_type=F32) for a in range(groups)]
        return jnp.concatenate(parts, axis=1) / scale

    def step(left):
        return 1.5 * left - 0.5 * image(left)

    share = rows // groups
    mine = lax.dynamic_slice_in_dim(every, me * share, share, 0).astype(F32)
    inner = step(image(step(mine)))
    white = step(1.5 * mine - 0.5 * inner) / jnp.sqrt(scale)
    white = white.astype(BF16).reshape(share, groups, cols)
    white = sent_parts(jnp.moveaxis(white, 1, 0), SAMP)
    return white.reshape(copies, snps, cols)


def solution(mesh):
    finer = Mesh(mesh.devices.reshape(2, 2, 4, 8, 2), (*SAMP, *SNP))
    in_specs = (P(SNP, SAMP), P(SAMP, None), P(None, SAMP), P(SNP))
    return jax.shard_map(
        shards, mesh=finer, in_specs=in_specs, out_specs=P(None, SNP, SAMP), check_vma=False
    )
```

```python
import functools

import jax
import jax.numpy as jnp
from jax import lax
from jax.experimental import pallas as pl
from jax.experimental.pallas import tpu as pltpu
from jax.sharding import Mesh
from jax.sharding import PartitionSpec as P

SAMP = ("y_lo", "core")
SNP = ("x", "z", "y_hi")
F32 = jnp.float32
BF16 = jnp.bfloat16
NT = (((1,), (1,)), ((), ()))
TN = (((0,), (0,)), ((), ()))
LOW = 256
MESH = pl.DeviceIdType.MESH
LANES = 128


def sent_parts(array, axis):
    return lax.all_to_all(array, axis, split_axis=0, concat_axis=0, tiled=True)


def copies_from(array, axis):
    devices = lax.axis_size(axis)
    return sent_parts(jnp.broadcast_to(array[None], (devices, *array.shape)), axis)


def spread_kernel(
    total, part, out, x_slots, pair, acc, slots, chunk,
    x_send, x_recv, r_send, r_recv, g_send, g_recv,
    xg_send, xg_recv, y_send, y_recv, c_send, c_recv, own_sem,
):
    rows, cols = part.shape
    block, half, bit = rows // 4, rows // 8, rows // 64
    x, z, y_hi = lax.axis_index("x"), lax.axis_index("z"), lax.axis_index("y_hi")
    y_lo, core = lax.axis_index("y_lo"), lax.axis_index("core")
    right, left, across = lax.rem(x + 1, 4), lax.rem(x + 3, 4), lax.rem(x + 2, 4)
    to_right, to_left = {"x": right}, {"x": left}
    sibling = {"core": 1 - core}
    near, far = {"y_lo": 1 - y_lo}, {"y_lo": 1 - y_lo, "y_hi": 1 - y_hi}
    peers = [(dz, dy) for dz in range(8) for dy in range(2) if dz or dy]

    def peer(dz, dy):
        there = {"z": lax.rem(z + dz, 8)}
        if dy:
            there["y_hi"] = 1 - y_hi
        return there

    barrier = pltpu.get_barrier_semaphore()
    greeted = [to_right, to_left, sibling, near, far] + [peer(*p) for p in peers]
    for there in greeted:
        pl.semaphore_signal(barrier, inc=1, device_id=there, device_id_type=MESH)
    pl.semaphore_wait(barrier, len(greeted))

    started = []

    def send(src, dst, send_sem, recv_sem, there):
        copy = pltpu.make_async_remote_copy(
            src_ref=src, dst_ref=dst, send_sem=send_sem, recv_sem=recv_sem,
            device_id=there, device_id_type=MESH,
        )
        copy.start()
        started.append(copy)
        return copy

    def half_of(owner, h):
        return part.at[pl.ds(pl.multiple_of(owner * block + h * half, half), half)]

    def x_sent(i, src, there):
        return send(src, x_slots.at[i], x_send.at[i], x_recv.at[i], there)

    hop_r = x_sent(0, half_of(across, 0), to_right)
    hop_l = x_sent(1, half_of(across, 1), to_left)
    own_r = x_sent(2, half_of(right, 1), to_right)
    own_l = x_sent(3, half_of(left, 0), to_left)

    def added(dst, sources):
        @pl.loop(0, half, step=32)
        def _(r):
            at = pl.ds(pl.multiple_of(r, 32), 32)
            value = sources[0][at, :].astype(F32)
            for source in sources[1:]:
                value += source[at, :].astype(F32)
            dst[at, :] = value.astype(BF16)

    hop_r.wait_recv()
    added(pair.at[0], [half_of(right, 0), x_slots.at[0]])
    sum_r = x_sent(4, pair.at[0], to_right)
    hop_l.wait_recv()
    added(pair.at[1], [half_of(left, 1), x_slots.at[1]])
    sum_l = x_sent(5, pair.at[1], to_left)
    own_l.wait_recv()
    sum_r.wait_recv()
    added(acc.at[pl.ds(0, half)], [half_of(x, 0), x_slots.at[3], x_slots.at[4]])
    own_r.wait_recv()
    sum_l.wait_recv()
    added(acc.at[pl.ds(half, half)], [half_of(x, 1), x_slots.at[2], x_slots.at[5]])

    def bit_at(at_y, at_z):
        return pl.ds(pl.multiple_of((at_y * 8 + at_z) * bit, bit), bit)

    arrive = []
    for i, (dz, dy) in enumerate(peers):
        at_y = 1 - y_hi if dy else y_hi
        arrive.append(
            send(
                acc.at[bit_at(at_y, lax.rem(z + dz, 8))], slots.at[i],
                r_send.at[i], r_recv.at[i], peer(dz, dy),
            )
        )
    value = acc[bit_at(y_hi, z), :].astype(F32)
    for i, copy in enumerate(arrive):
        copy.wait_recv()
        value += slots[i].astype(F32)
    chunk[...] = (value / total).astype(BF16)

    piece = y_lo * 2 + core
    mine = pl.ds(pl.multiple_of(x * block + (y_hi * 8 + z) * bit, bit), bit)
    stay = pltpu.make_async_copy(chunk, out.at[piece, mine], own_sem)
    stay.start()
    arrive = []
    for i, (dz, dy) in enumerate(peers):
        arrive.append(
            send(chunk, out.at[piece, mine], g_send.at[i], g_recv.at[i], peer(dz, dy))
        )
    stay.wait()
    for copy in arrive:
        copy.wait_recv()

    def at_half(which, owner, h):
        return out.at[which, pl.ds(pl.multiple_of(owner * block + h * half, half), half)]

    def at_block(which, owner):
        return out.at[which, pl.ds(pl.multiple_of(owner * block, block), block)]

    def passed(src, sems, i, there):
        return send(src, src, sems[0].at[i], sems[1].at[i], there)

    xs, ys, cs = (xg_send, xg_recv), (y_send, y_recv), (c_send, c_recv)

    def to_y(i, owner):
        return (
            passed(at_half(piece, owner, 0), ys, 2 * i, near),
            passed(at_half(piece, owner, 1), ys, 2 * i + 1, far),
        )

    go_r = passed(at_block(piece, x), xs, 0, to_right)
    go_l = passed(at_block(piece, x), xs, 1, to_left)
    y_own = to_y(0, x)
    c_all = [passed(at_block(piece, x), cs, 0, sibling)]
    go_r.wait_recv()
    hop_r = passed(at_half(piece, left, 0), xs, 2, to_right)
    y_left = to_y(1, left)
    go_l.wait_recv()
    hop_l = passed(at_half(piece, right, 1), xs, 3, to_left)
    y_right = to_y(2, right)
    c_all.append(passed(at_block(piece, left), cs, 1, sibling))
    c_all.append(passed(at_block(piece, right), cs, 2, sibling))
    other = (1 - y_lo) * 2 + core

    def from_y(copies, owner, i):
        for h, copy in enumerate(copies):
            copy.wait_recv()
        c_all.append(passed(at_block(other, owner), cs, i, sibling))

    from_y(y_own, x, 3)
    hop_r.wait_recv()
    y_far = [passed(at_half(piece, across, 0), ys, 6, near)]
    hop_l.wait_recv()
    y_far.append(passed(at_half(piece, across, 1), ys, 7, far))
    c_all.append(passed(at_block(piece, across), cs, 4, sibling))
    from_y(y_left, left, 5)
    from_y(y_right, right, 6)
    from_y(y_far, across, 7)
    for copy in c_all:
        copy.wait_recv()
    for copy in started:
        copy.wait_send()


def spread(part, total):
    rows, cols = part.shape
    dma = pltpu.SemaphoreType.DMA
    pairs = [6, 6, 15, 15, 15, 15, 4, 4, 8, 8, 8, 8]
    return pl.pallas_call(
        functools.partial(spread_kernel, total),
        out_shape=jax.ShapeDtypeStruct((4, rows, cols), BF16),
        in_specs=[pl.BlockSpec(memory_space=pltpu.VMEM)],
        out_specs=pl.BlockSpec(memory_space=pl.ANY),
        scratch_shapes=[
            pltpu.VMEM((6, rows // 8, cols), BF16),
            pltpu.VMEM((2, rows // 8, cols), BF16),
            pltpu.VMEM((rows // 4, cols), BF16),
            pltpu.VMEM((15, rows // 64, cols), BF16),
            pltpu.VMEM((rows // 64, cols), BF16),
            *[dma((n,)) for n in pairs],
            dma,
        ],
        compiler_params=pltpu.CompilerParams(
            collective_id=0, has_side_effects=True, vmem_limit_bytes=32 << 20
        ),
        name="sum_and_spread",
    )(part)


def apply_kernel(genes, gram, start, out, first, left):
    pieces, rows, width = gram.shape
    block = rows // 2
    trace = F32(0)
    for a in range(pieces):
        h, o = a // 2, (a % 2) * block
        tile = gram[a, h * block : (h + 1) * block, o : o + block].astype(F32)
        spot = lax.broadcasted_iota(jnp.int32, tile.shape, 0)
        spot = spot == lax.broadcasted_iota(jnp.int32, tile.shape, 1)
        trace += jnp.sum(jnp.where(spot, tile, F32(0)))
    scale = jnp.full((1, LANES), trace / genes + 1e-06, F32)
    inverse = 1.0 / scale
    rsqrt = 1.0 / jnp.sqrt(scale)

    def image(a):
        value = jnp.dot(gram[a, :block], left[:width], preferred_element_type=F32)
        value += jnp.dot(gram[a, block:], left[width:], preferred_element_type=F32)
        return value * inverse

    left[...] = start[...]

    @pl.loop(0, pieces)
    def _(a):
        at = pl.ds(pl.multiple_of(a * block, block), block)
        first[at, :] = (1.5 * start[at, :].astype(F32) - 0.5 * image(a)).astype(BF16)

    left[...] = first[...]

    @pl.loop(0, pieces)
    def _(a):
        at = pl.ds(pl.multiple_of(a * block, block), block)
        first[at, :] = image(a).astype(BF16)

    left[...] = first[...]

    @pl.loop(0, pieces)
    def _(a):
        at = pl.ds(pl.multiple_of(a * block, block), block)
        inner = 1.5 * left[at, :].astype(F32) - 0.5 * image(a)
        first[at, :] = (1.5 * start[at, :].astype(F32) - 0.5 * inner).astype(BF16)

    left[...] = first[...]

    @pl.loop(0, pieces)
    def _(a):
        at = pl.ds(pl.multiple_of(a * block, block), block)
        value = 1.5 * left[at, :].astype(F32) - 0.5 * image(a)
        out[at, :] = (value * rsqrt).astype(BF16)


def applied(gram, start, genes):
    vmem = pl.BlockSpec(memory_space=pltpu.VMEM)
    return pl.pallas_call(
        functools.partial(apply_kernel, genes),
        out_shape=jax.ShapeDtypeStruct(start.shape, BF16),
        in_specs=[vmem, vmem],
        out_specs=vmem,
        scratch_shapes=[pltpu.VMEM(start.shape, BF16)] * 2,
        compiler_params=pltpu.CompilerParams(vmem_limit_bytes=48 << 20),
        name="whiten_rows",
    )(gram, start)


def shards(dosage, pheno, perm, snp_weight):
    snps, own = dosage.shape
    genes = pheno.shape[1]
    groups = lax.axis_size(SAMP)
    samples = own * groups
    total_snps = snps * lax.axis_size(SNP)
    nulls = perm.shape[0]
    copies = nulls + 1
    rows = copies * snps
    cols = genes // groups
    me = lax.axis_index(SAMP)
    coded = jnp.concatenate(
        [dosage, perm // LOW, perm % LOW], axis=0
    ).astype(BF16)
    coded = copies_from(coded, SAMP)
    coded = jnp.moveaxis(coded, 0, 1).reshape(coded.shape[1], samples)
    pheno_parts = jnp.moveaxis(pheno.reshape(own, groups, cols), 1, 0)
    pheno_cols = sent_parts(pheno_parts, SAMP).reshape(samples, cols)
    dose = coded[:snps]
    high = coded[snps : snps + nulls]
    low = coded[snps + nulls :]
    steps = samples // LOW
    step_ids = jnp.arange(steps).astype(BF16)[:, None, None]
    low_ids = jnp.arange(LOW).astype(BF16)[:, None]
    placed = [dose]
    for k in range(nulls):
        masked = jnp.where(high[k][None, None, :] == step_ids, dose[None], jnp.zeros((), BF16))
        onehot = (low[k][None, :] == low_ids).astype(BF16)
        part = lax.dot_general(
            masked.reshape(steps * snps, samples), onehot, NT, preferred_element_type=F32
        ).astype(BF16)
        part = part.reshape(steps, snps, LOW)
        placed.append(jnp.concatenate([part[h] for h in range(steps)], axis=1))
    placed = jnp.concatenate(placed, axis=0)
    raw = jnp.dot(placed, pheno_cols, preferred_element_type=F32)
    dose32 = dose.astype(F32)
    dose_mean = jnp.sum(dose32, axis=1) / samples
    dose_square = jnp.sum(dose32 * dose32, axis=1) / samples
    pheno_sum = jnp.sum(pheno_cols.astype(F32), axis=0)
    spread_rows = jnp.sqrt(samples * (dose_square + 1e-05))
    mean_rows = jnp.tile(dose_mean, copies)[:, None]
    spread_rows = jnp.tile(spread_rows, copies)[:, None]
    scores = ((raw - mean_rows * pheno_sum[None, :]) / spread_rows).astype(BF16)
    every = copies_from(scores, SAMP)
    every = jnp.moveaxis(every, 0, 1).reshape(rows, genes)
    weight_rows = jnp.tile(snp_weight, nulls)[:, None]
    weighted = (every[snps:].astype(F32) * weight_rows).astype(BF16)
    width = genes // 2
    part = jnp.concatenate(
        [
            lax.dot_general(
                scores[snps:], weighted[:, h * width : (h + 1) * width], TN,
                preferred_element_type=F32,
            ).astype(BF16)
            for h in range(2)
        ],
        axis=0,
    )
    gram = spread(part, nulls * total_snps)
    share = rows // groups
    mine = lax.dynamic_slice_in_dim(every, me * share, share, 0)
    start = jnp.pad(mine.T, ((0, 0), (0, LANES - share)))
    white = applied(gram, start, genes)[:, :share].T
    white = white.reshape(share, groups, cols)
    white = sent_parts(jnp.moveaxis(white, 1, 0), SAMP)
    return white.reshape(copies, snps, cols)


def solution(mesh):
    finer = Mesh(mesh.devices.reshape(2, 2, 4, 8, 2), (*SAMP, *SNP))
    in_specs = (P(SNP, SAMP), P(SAMP, None), P(None, SAMP), P(SNP))
    return jax.shard_map(
        shards, mesh=finer, in_specs=in_specs, out_specs=P(None, SNP, SAMP), check_vma=False
    )
```

```python
import functools

import jax
import jax.numpy as jnp
from jax import lax
from jax.experimental import pallas as pl
from jax.experimental.pallas import tpu as pltpu
from jax.sharding import Mesh
from jax.sharding import PartitionSpec as P

SAMP = ("y_lo", "core")
SNP = ("x", "z", "y_hi")
F32 = jnp.float32
BF16 = jnp.bfloat16
NT = (((1,), (1,)), ((), ()))
LOW = 256
MESH = pl.DeviceIdType.MESH
LANES = 128


def sent_parts(array, axis):
    return lax.all_to_all(array, axis, split_axis=0, concat_axis=0, tiled=True)


def spread_kernel(
    total, part, out, x_slots, pair, acc, slots, chunk,
    x_send, x_recv, r_send, r_recv, g_send, g_recv,
    xg_send, xg_recv, y_send, y_recv, c_send, c_recv, own_sem,
):
    rows, cols = part.shape
    block, half, bit = rows // 4, rows // 8, rows // 64
    x, z, y_hi = lax.axis_index("x"), lax.axis_index("z"), lax.axis_index("y_hi")
    y_lo, core = lax.axis_index("y_lo"), lax.axis_index("core")
    right, left, across = lax.rem(x + 1, 4), lax.rem(x + 3, 4), lax.rem(x + 2, 4)
    to_right, to_left = {"x": right}, {"x": left}
    sibling = {"core": 1 - core}
    near, far = {"y_lo": 1 - y_lo}, {"y_lo": 1 - y_lo, "y_hi": 1 - y_hi}
    peers = [(dz, dy) for dz in range(8) for dy in range(2) if dz or dy]

    def peer(dz, dy):
        there = {"z": lax.rem(z + dz, 8)}
        if dy:
            there["y_hi"] = 1 - y_hi
        return there

    barrier = pltpu.get_barrier_semaphore()
    greeted = [to_right, to_left, sibling, near, far] + [peer(*p) for p in peers]
    for there in greeted:
        pl.semaphore_signal(barrier, inc=1, device_id=there, device_id_type=MESH)
    pl.semaphore_wait(barrier, len(greeted))

    started = []

    def send(src, dst, send_sem, recv_sem, there):
        copy = pltpu.make_async_remote_copy(
            src_ref=src, dst_ref=dst, send_sem=send_sem, recv_sem=recv_sem,
            device_id=there, device_id_type=MESH,
        )
        copy.start()
        started.append(copy)
        return copy

    def half_of(owner, h):
        return part.at[pl.ds(pl.multiple_of(owner * block + h * half, half), half)]

    def x_sent(i, src, there):
        return send(src, x_slots.at[i], x_send.at[i], x_recv.at[i], there)

    hop_r = x_sent(0, half_of(across, 0), to_right)
    hop_l = x_sent(1, half_of(across, 1), to_left)
    own_r = x_sent(2, half_of(right, 1), to_right)
    own_l = x_sent(3, half_of(left, 0), to_left)

    def added(dst, sources):
        @pl.loop(0, half, step=32)
        def _(r):
            at = pl.ds(pl.multiple_of(r, 32), 32)
            value = sources[0][at, :].astype(F32)
            for source in sources[1:]:
                value += source[at, :].astype(F32)
            dst[at, :] = value.astype(BF16)

    hop_r.wait_recv()
    added(pair.at[0], [half_of(right, 0), x_slots.at[0]])
    sum_r = x_sent(4, pair.at[0], to_right)
    hop_l.wait_recv()
    added(pair.at[1], [half_of(left, 1), x_slots.at[1]])
    sum_l = x_sent(5, pair.at[1], to_left)
    own_l.wait_recv()
    sum_r.wait_recv()
    added(acc.at[pl.ds(0, half)], [half_of(x, 0), x_slots.at[3], x_slots.at[4]])
    own_r.wait_recv()
    sum_l.wait_recv()
    added(acc.at[pl.ds(half, half)], [half_of(x, 1), x_slots.at[2], x_slots.at[5]])

    def bit_at(at_y, at_z):
        return pl.ds(pl.multiple_of((at_y * 8 + at_z) * bit, bit), bit)

    arrive = []
    for i, (dz, dy) in enumerate(peers):
        at_y = 1 - y_hi if dy else y_hi
        arrive.append(
            send(
                acc.at[bit_at(at_y, lax.rem(z + dz, 8))], slots.at[i],
                r_send.at[i], r_recv.at[i], peer(dz, dy),
            )
        )
    value = acc[bit_at(y_hi, z), :].astype(F32)
    for i, copy in enumerate(arrive):
        copy.wait_recv()
        value += slots[i].astype(F32)
    chunk[...] = (value / total).astype(BF16)

    piece = y_lo * 2 + core
    mine = pl.ds(pl.multiple_of(x * block + (y_hi * 8 + z) * bit, bit), bit)
    stay = pltpu.make_async_copy(chunk, out.at[piece, mine], own_sem)
    stay.start()
    arrive = []
    for i, (dz, dy) in enumerate(peers):
        arrive.append(
            send(chunk, out.at[piece, mine], g_send.at[i], g_recv.at[i], peer(dz, dy))
        )
    stay.wait()
    for copy in arrive:
        copy.wait_recv()

    def at_half(which, owner, h):
        return out.at[which, pl.ds(pl.multiple_of(owner * block + h * half, half), half)]

    def at_block(which, owner):
        return out.at[which, pl.ds(pl.multiple_of(owner * block, block), block)]

    def passed(src, sems, i, there):
        return send(src, src, sems[0].at[i], sems[1].at[i], there)

    xs, ys, cs = (xg_send, xg_recv), (y_send, y_recv), (c_send, c_recv)

    def to_y(i, owner):
        return (
            passed(at_half(piece, owner, 0), ys, 2 * i, near),
            passed(at_half(piece, owner, 1), ys, 2 * i + 1, far),
        )

    go_r = passed(at_block(piece, x), xs, 0, to_right)
    go_l = passed(at_block(piece, x), xs, 1, to_left)
    y_own = to_y(0, x)
    c_all = [passed(at_block(piece, x), cs, 0, sibling)]
    go_r.wait_recv()
    hop_r = passed(at_half(piece, left, 0), xs, 2, to_right)
    y_left = to_y(1, left)
    go_l.wait_recv()
    hop_l = passed(at_half(piece, right, 1), xs, 3, to_left)
    y_right = to_y(2, right)
    c_all.append(passed(at_block(piece, left), cs, 1, sibling))
    c_all.append(passed(at_block(piece, right), cs, 2, sibling))
    other = (1 - y_lo) * 2 + core

    def from_y(copies, owner, i):
        for h, copy in enumerate(copies):
            copy.wait_recv()
        c_all.append(passed(at_block(other, owner), cs, i, sibling))

    from_y(y_own, x, 3)
    hop_r.wait_recv()
    y_far = [passed(at_half(piece, across, 0), ys, 6, near)]
    hop_l.wait_recv()
    y_far.append(passed(at_half(piece, across, 1), ys, 7, far))
    c_all.append(passed(at_block(piece, across), cs, 4, sibling))
    from_y(y_left, left, 5)
    from_y(y_right, right, 6)
    from_y(y_far, across, 7)
    for copy in c_all:
        copy.wait_recv()
    for copy in started:
        copy.wait_send()


def spread(part, total):
    rows, cols = part.shape
    dma = pltpu.SemaphoreType.DMA
    pairs = [6, 6, 15, 15, 15, 15, 4, 4, 8, 8, 8, 8]
    return pl.pallas_call(
        functools.partial(spread_kernel, total),
        out_shape=jax.ShapeDtypeStruct((4, rows, cols), BF16),
        in_specs=[pl.BlockSpec(memory_space=pltpu.VMEM)],
        out_specs=pl.BlockSpec(memory_space=pl.ANY),
        scratch_shapes=[
            pltpu.VMEM((6, rows // 8, cols), BF16),
            pltpu.VMEM((2, rows // 8, cols), BF16),
            pltpu.VMEM((rows // 4, cols), BF16),
            pltpu.VMEM((15, rows // 64, cols), BF16),
            pltpu.VMEM((rows // 64, cols), BF16),
            *[dma((n,)) for n in pairs],
            dma,
        ],
        compiler_params=pltpu.CompilerParams(
            collective_id=0, has_side_effects=True, vmem_limit_bytes=32 << 20
        ),
        name="sum_and_spread",
    )(part)


def front_kernel(
    dosage, pheno, perm, weight_rows, part, every,
    coded, codes, placed, cols_in, turned,
    a_send, a_recv, p_send, p_recv, s_send, s_recv, n_send, n_recv, f_send, f_recv, own_sem,
):
    snps, own = dosage.shape
    nulls = perm.shape[0]
    samples, cols = cols_in.shape
    copies = nulls + 1
    rows = copies * snps
    lead = placed.shape[0] - rows
    y_lo, core, y_hi = lax.axis_index("y_lo"), lax.axis_index("core"), lax.axis_index("y_hi")
    me = y_lo * 2 + core
    sib_id = y_lo * 2 + 1 - core
    near_id = (1 - y_lo) * 2 + core
    cross_id = (1 - y_lo) * 2 + 1 - core
    sibling = {"core": 1 - core}
    near = {"y_lo": 1 - y_lo}
    cross = {"y_lo": 1 - y_lo, "core": 1 - core}
    far = {"y_lo": 1 - y_lo, "y_hi": 1 - y_hi}
    far_cross = {"y_lo": 1 - y_lo, "y_hi": 1 - y_hi, "core": 1 - core}

    def span(index, size):
        return pl.ds(pl.multiple_of(index * size, size), size)

    barrier = pltpu.get_barrier_semaphore()
    greeted = (sibling, near, cross, far, far_cross)
    for there in greeted:
        pl.semaphore_signal(barrier, inc=1, device_id=there, device_id_type=MESH)
    mine = span(me, own)
    coded[:snps, mine] = dosage[...].astype(F32).astype(BF16)
    source = perm[...]
    both = jnp.concatenate([lax.shift_right_logical(source, 8), source & 255], axis=0)
    coded[snps:, mine] = both.astype(F32).astype(BF16)
    pl.semaphore_wait(barrier, len(greeted))

    started = []

    def send(src, dst, send_sem, recv_sem, there):
        copy = pltpu.make_async_remote_copy(
            src_ref=src, dst_ref=dst, send_sem=send_sem, recv_sem=recv_sem,
            device_id=there, device_id_type=MESH,
        )
        copy.start()
        started.append(copy)
        return copy

    coming = [
        send(coded.at[:, mine], coded.at[:, mine], a_send.at[i], a_recv.at[i], there)
        for i, there in enumerate((near, cross, sibling))
    ]
    half = own // 2
    pheno_coming = []
    for i, (there, target, h) in enumerate(
        ((near, near_id, 0), (cross, cross_id, 0), (far, near_id, 1), (far_cross, cross_id, 1))
    ):
        pheno_coming.append(
            send(
                pheno.at[pl.ds(h * half, half), span(target, cols)],
                cols_in.at[pl.ds(pl.multiple_of(me * own + h * half, half), half)],
                p_send.at[i], p_recv.at[i], there,
            )
        )
    pheno_coming.append(
        send(
            pheno.at[:, span(sib_id, cols)], cols_in.at[span(me, own)],
            p_send.at[4], p_recv.at[4], sibling,
        )
    )
    stay = pltpu.make_async_copy(pheno.at[:, span(me, cols)], cols_in.at[span(me, own)], own_sem)
    stay.start()
    placed[:lead, :] = jnp.ones((lead, samples), BF16)
    for copy in coming:
        copy.wait_recv()

    codes[...] = coded[snps:, :].astype(F32)
    dose = coded[:snps, :]
    placed[lead : lead + snps, :] = dose
    dose32 = dose.astype(F32)
    dose_mean = jnp.sum(dose32, axis=1, keepdims=True) / samples
    dose_square = jnp.sum(dose32 * dose32, axis=1, keepdims=True) / samples
    spread_rows = jnp.sqrt(samples * (dose_square + 1e-05))
    steps = samples // LOW

    @pl.loop(0, nulls)
    def _(k):
        high = codes[pl.ds(k, 1), :]
        low = codes[pl.ds(nulls + k, 1), :]
        values = coded[:snps, :]
        masked = jnp.concatenate(
            [values * (high == F32(h)).astype(F32).astype(BF16) for h in range(steps)], axis=0
        )
        ids = lax.broadcasted_iota(jnp.int32, (LOW, samples), 0).astype(F32)
        onehot = (ids == low).astype(F32).astype(BF16)
        got = lax.dot_general(masked, onehot, NT, preferred_element_type=F32).astype(BF16)
        at = pl.ds(pl.multiple_of(lead + (k + 1) * snps, 16), snps)
        for h in range(steps):
            placed[at, h * LOW : (h + 1) * LOW] = got[h * snps : (h + 1) * snps]

    stay.wait()
    for copy in pheno_coming:
        copy.wait_recv()

    chunks = 3
    per = copies // chunks
    total = None
    to_sib, to_near = [], []
    for c in range(chunks):
        first = 0 if c == 0 else lead + c * per * snps
        last = lead + (c + 1) * per * snps
        raw = jnp.dot(placed[first:last, :], cols_in[...], preferred_element_type=F32)
        if c == 0:
            total = raw[:1]
            raw = raw[lead:]
        for j in range(per):
            value = (raw[j * snps : (j + 1) * snps] - dose_mean * total) / spread_rows
            at = (c * per + j) * snps
            every[me, at : at + snps] = value.astype(BF16)
        sent = pl.ds(c * per * snps, per * snps)
        block = every.at[me, sent]
        to_near.append(send(block, block, n_send.at[c], n_recv.at[c], near))
        to_sib.append(send(block, block, s_send.at[c], s_recv.at[c], sibling))

    turned[...] = every[me, snps:].astype(F32).T.astype(BF16)

    def share(which):
        weighted = (every[which, snps:].astype(F32) * weight_rows[...]).astype(BF16)
        part[span(which, cols), :] = jnp.dot(
            turned[...], weighted, preferred_element_type=F32
        ).astype(BF16)

    share(me)
    for copy in to_sib:
        copy.wait_recv()
    share(sib_id)
    passed = []
    for c in range(chunks):
        to_near[c].wait_recv()
        block = every.at[near_id, pl.ds(c * per * snps, per * snps)]
        passed.append(send(block, block, f_send.at[c], f_recv.at[c], sibling))
    share(near_id)
    for copy in passed:
        copy.wait_recv()
    share(cross_id)
    for copy in started:
        copy.wait_send()


def front(dosage, pheno, perm, weight_rows):
    snps, own = dosage.shape
    genes = pheno.shape[1]
    nulls = perm.shape[0]
    rows = (nulls + 1) * snps
    samples, cols = own * 4, genes // 4
    lead = 16
    dma = pltpu.SemaphoreType.DMA
    vmem = pl.BlockSpec(memory_space=pltpu.VMEM)
    pairs = [3, 3, 5, 5, 3, 3, 3, 3, 3, 3]
    return pl.pallas_call(
        front_kernel,
        out_shape=(
            jax.ShapeDtypeStruct((genes, cols), BF16),
            jax.ShapeDtypeStruct((4, rows, cols), BF16),
        ),
        in_specs=[vmem, pl.BlockSpec(memory_space=pl.ANY), vmem, vmem],
        out_specs=(vmem, vmem),
        scratch_shapes=[
            pltpu.VMEM((snps + 2 * nulls, samples), BF16),
            pltpu.VMEM((2 * nulls, samples), F32),
            pltpu.VMEM((lead + rows, samples), BF16),
            pltpu.VMEM((samples, cols), BF16),
            pltpu.VMEM((cols, rows - snps), BF16),
            *[dma((n,)) for n in pairs],
            dma,
        ],
        compiler_params=pltpu.CompilerParams(
            collective_id=1, has_side_effects=True, vmem_limit_bytes=40 << 20
        ),
        name="scores_and_gram_share",
    )(dosage, pheno, perm, weight_rows)


def apply_kernel(genes, gram, start, out, first, left):
    pieces, rows, block = gram.shape
    trace = F32(0)
    for a in range(pieces):
        tile = gram[a, a * block : (a + 1) * block].astype(F32)
        spot = lax.broadcasted_iota(jnp.int32, tile.shape, 0)
        spot = spot == lax.broadcasted_iota(jnp.int32, tile.shape, 1)
        trace += jnp.sum(jnp.where(spot, tile, F32(0)))
    scale = jnp.full((1, LANES), trace / genes + 1e-06, F32)
    inverse = 1.0 / scale
    rsqrt = 1.0 / jnp.sqrt(scale)

    def image(a):
        value = None
        for b in range(pieces):
            at = slice(b * block, (b + 1) * block)
            one = jnp.dot(gram[a, at], left[at], preferred_element_type=F32)
            value = one if value is None else value + one
        return value * inverse

    left[...] = start[...]

    @pl.loop(0, pieces)
    def _(a):
        at = pl.ds(pl.multiple_of(a * block, block), block)
        first[at, :] = (1.5 * start[at, :].astype(F32) - 0.5 * image(a)).astype(BF16)

    left[...] = first[...]

    @pl.loop(0, pieces)
    def _(a):
        at = pl.ds(pl.multiple_of(a * block, block), block)
        first[at, :] = image(a).astype(BF16)

    left[...] = first[...]

    @pl.loop(0, pieces)
    def _(a):
        at = pl.ds(pl.multiple_of(a * block, block), block)
        inner = 1.5 * left[at, :].astype(F32) - 0.5 * image(a)
        first[at, :] = (1.5 * start[at, :].astype(F32) - 0.5 * inner).astype(BF16)

    left[...] = first[...]

    @pl.loop(0, pieces)
    def _(a):
        at = pl.ds(pl.multiple_of(a * block, block), block)
        value = 1.5 * left[at, :].astype(F32) - 0.5 * image(a)
        out[at, :] = (value * rsqrt).astype(BF16)


def applied(gram, start, genes):
    vmem = pl.BlockSpec(memory_space=pltpu.VMEM)
    return pl.pallas_call(
        functools.partial(apply_kernel, genes),
        out_shape=jax.ShapeDtypeStruct(start.shape, BF16),
        in_specs=[vmem, vmem],
        out_specs=vmem,
        scratch_shapes=[pltpu.VMEM(start.shape, BF16)] * 2,
        compiler_params=pltpu.CompilerParams(vmem_limit_bytes=48 << 20),
        name="whiten_rows",
    )(gram, start)


def shards(dosage, pheno, perm, snp_weight):
    snps = dosage.shape[0]
    genes = pheno.shape[1]
    groups = lax.axis_size(SAMP)
    nulls = perm.shape[0]
    copies = nulls + 1
    rows = copies * snps
    cols = genes // groups
    me = lax.axis_index(SAMP)
    weight_rows = jnp.tile(snp_weight, nulls)[:, None]
    part, every = front(dosage, pheno, perm, weight_rows)
    gram = spread(part, nulls * snps * lax.axis_size(SNP))
    share = rows // groups
    mine = lax.dynamic_slice_in_dim(every, me * share, share, 1)
    start = jnp.swapaxes(mine, 1, 2).reshape(genes, share)
    start = jnp.pad(start, ((0, 0), (0, LANES - share)))
    white = applied(gram, start, genes)[:, :share].T
    white = white.reshape(share, groups, cols)
    white = sent_parts(jnp.moveaxis(white, 1, 0), SAMP)
    return white.reshape(copies, snps, cols)


def solution(mesh):
    finer = Mesh(mesh.devices.reshape(2, 2, 4, 8, 2), (*SAMP, *SNP))
    in_specs = (P(SNP, SAMP), P(SAMP, None), P(None, SAMP), P(SNP))
    return jax.shard_map(
        shards, mesh=finer, in_specs=in_specs, out_specs=P(None, SNP, SAMP), check_vma=False
    )
```

```python
import functools

import jax
import jax.numpy as jnp
from jax import lax
from jax.experimental import pallas as pl
from jax.experimental.pallas import tpu as pltpu
from jax.sharding import Mesh
from jax.sharding import PartitionSpec as P

SAMP = ("y_lo", "core")
SNP = ("x", "z", "y_hi")
F32 = jnp.float32
BF16 = jnp.bfloat16
NT = (((1,), (1,)), ((), ()))
LOW = 256
TILE = 256
WIDE = 640
LANES = 128
LEAD = 16
CHUNKS = 3
MESH = pl.DeviceIdType.MESH


def span(index, size):
    return pl.ds(pl.multiple_of(index * size, size), size)


class Sender:
    def __init__(self):
        self.started = []

    def __call__(self, src, dst, sems, i, there):
        copy = pltpu.make_async_remote_copy(
            src_ref=src, dst_ref=dst, send_sem=sems[0].at[i], recv_sem=sems[1].at[i],
            device_id=there, device_id_type=MESH,
        )
        copy.start()
        self.started.append(copy)
        return copy

    def finish(self):
        for copy in self.started:
            copy.wait_send()


class Place:
    def __init__(self):
        x, z, y_hi = lax.axis_index("x"), lax.axis_index("z"), lax.axis_index("y_hi")
        y_lo, core = lax.axis_index("y_lo"), lax.axis_index("core")
        self.x, self.z, self.y_hi, self.y_lo, self.core = x, z, y_hi, y_lo, core
        self.me = y_lo * 2 + core
        self.sib_id = y_lo * 2 + 1 - core
        self.near_id = (1 - y_lo) * 2 + core
        self.cross_id = (1 - y_lo) * 2 + 1 - core
        self.sibling = {"core": 1 - core}
        self.near = {"y_lo": 1 - y_lo}
        self.cross = {"y_lo": 1 - y_lo, "core": 1 - core}
        self.far = {"y_lo": 1 - y_lo, "y_hi": 1 - y_hi}
        self.far_cross = {"y_lo": 1 - y_lo, "y_hi": 1 - y_hi, "core": 1 - core}
        self.right, self.left = lax.rem(x + 1, 4), lax.rem(x + 3, 4)
        self.across = lax.rem(x + 2, 4)
        self.to_right, self.to_left = {"x": self.right}, {"x": self.left}
        self.peers = [(dz, dy) for dz in range(8) for dy in range(2) if dz or dy]

    def peer(self, dz, dy):
        there = {"z": lax.rem(self.z + dz, 8)}
        if dy:
            there["y_hi"] = 1 - self.y_hi
        return there


def score_steps(at, send, dosage, pheno, weight_rows, part, every, scratch):
    coded, codes, placed, cols_in, turned, near_w, a, p, s, n, f, own_sem = scratch
    snps, own = dosage.shape
    samples, cols = cols_in.shape
    nulls = codes.shape[0] // 2
    copies = nulls + 1
    mine = span(at.me, own)
    coming = [
        send(coded.at[:, mine], coded.at[:, mine], a, i, there)
        for i, there in enumerate((at.near, at.cross, at.sibling))
    ]
    half = own // 2
    pheno_coming = []
    for i, (there, target, h) in enumerate(
        (
            (at.near, at.near_id, 0), (at.cross, at.cross_id, 0),
            (at.far, at.near_id, 1), (at.far_cross, at.cross_id, 1),
        )
    ):
        pheno_coming.append(
            send(
                pheno.at[pl.ds(h * half, half), span(target, cols)],
                cols_in.at[pl.ds(pl.multiple_of(at.me * own + h * half, half), half)],
                p, i, there,
            )
        )
    pheno_coming.append(
        send(pheno.at[:, span(at.sib_id, cols)], cols_in.at[mine], p, 4, at.sibling)
    )
    stay = pltpu.make_async_copy(pheno.at[:, span(at.me, cols)], cols_in.at[mine], own_sem)
    stay.start()
    placed[:LEAD, :] = jnp.ones((LEAD, samples), BF16)
    for owner in range(4):
        every[owner, copies * snps :] = jnp.zeros((every.shape[1] - copies * snps, cols), BF16)
    for copy in coming:
        copy.wait_recv()

    codes[...] = coded[snps:, :].astype(F32)
    dose = coded[:snps, :]
    placed[LEAD : LEAD + snps, :] = dose
    dose32 = dose.astype(F32)
    dose_mean = jnp.sum(dose32, axis=1, keepdims=True) / samples
    dose_square = jnp.sum(dose32 * dose32, axis=1, keepdims=True) / samples
    spread_rows = jnp.sqrt(samples * (dose_square + 1e-05))
    steps = samples // LOW

    @pl.loop(0, nulls)
    def _(k):
        high = codes[pl.ds(k, 1), :]
        low = codes[pl.ds(nulls + k, 1), :]
        values = coded[:snps, :]
        masked = jnp.concatenate(
            [values * (high == F32(h)).astype(F32).astype(BF16) for h in range(steps)], axis=0
        )
        ids = lax.broadcasted_iota(jnp.int32, (LOW, samples), 0).astype(F32)
        onehot = (ids == low).astype(F32).astype(BF16)
        got = lax.dot_general(masked, onehot, NT, preferred_element_type=F32).astype(BF16)
        rows = pl.ds(pl.multiple_of(LEAD + (k + 1) * snps, 16), snps)
        for h in range(steps):
            placed[rows, h * LOW : (h + 1) * LOW] = got[h * snps : (h + 1) * snps]

    stay.wait()
    for copy in pheno_coming:
        copy.wait_recv()

    per = copies // CHUNKS
    total = None
    to_sib, to_near = [], []
    for c in range(CHUNKS):
        first = 0 if c == 0 else LEAD + c * per * snps
        last = LEAD + (c + 1) * per * snps
        raw = jnp.dot(placed[first:last, :], cols_in[...], preferred_element_type=F32)
        if c == 0:
            total = raw[:1]
            raw = raw[LEAD:]
        for j in range(per):
            value = (raw[j * snps : (j + 1) * snps] - dose_mean * total) / spread_rows
            row = (c * per + j) * snps
            every[at.me, row : row + snps] = value.astype(BF16)
        block = every.at[at.me, pl.ds(c * per * snps, per * snps)]
        to_near.append(send(block, block, n, c, at.near))
        to_sib.append(send(block, block, s, c, at.sibling))

    end = copies * snps
    turned[...] = every[at.me, snps:end].astype(F32).T.astype(BF16)
    passed = []
    for c in range(CHUNKS):
        to_near[c].wait_recv()
        block = every.at[at.near_id, pl.ds(c * per * snps, per * snps)]
        passed.append(send(block, block, f, c, at.sibling))
    for copy in to_sib + passed:
        copy.wait_recv()
    for r in range(3):
        value = every[lax.rem(at.me + r, 4), snps:end].astype(F32) * weight_rows[...]
        near_w[:, r * cols : (r + 1) * cols] = value.astype(BF16)
    for i in range(2):
        for h in range(2):
            row, first = (i * 2 + h) * TILE, i * TILE + h * WIDE
            part[row : row + TILE, :] = jnp.dot(
                turned[i * TILE : (i + 1) * TILE, :], near_w[:, first : first + WIDE],
                preferred_element_type=F32,
            ).astype(BF16)


def spread_steps(at, send, total, part, gram, scratch):
    x_slots, pair, acc, slots, chunk, xr, rr, gr, xg, ys, cs = scratch
    rows = part.shape[0]
    block, half, bit = rows // 4, rows // 8, rows // 64
    x, z, y_hi = at.x, at.z, at.y_hi
    right, left, across = at.right, at.left, at.across

    def half_of(owner, h):
        return part.at[pl.ds(pl.multiple_of(owner * block + h * half, half), half)]

    def x_sent(i, src, there):
        return send(src, x_slots.at[i], xr, i, there)

    hop_r = x_sent(0, half_of(across, 0), at.to_right)
    hop_l = x_sent(1, half_of(across, 1), at.to_left)
    own_r = x_sent(2, half_of(right, 1), at.to_right)
    own_l = x_sent(3, half_of(left, 0), at.to_left)

    def added(dst, sources):
        @pl.loop(0, half, step=32)
        def _(r):
            rows_at = pl.ds(pl.multiple_of(r, 32), 32)
            value = sources[0][rows_at, :].astype(F32)
            for source in sources[1:]:
                value += source[rows_at, :].astype(F32)
            dst[rows_at, :] = value.astype(BF16)

    hop_r.wait_recv()
    added(pair.at[0], [half_of(right, 0), x_slots.at[0]])
    sum_r = x_sent(4, pair.at[0], at.to_right)
    hop_l.wait_recv()
    added(pair.at[1], [half_of(left, 1), x_slots.at[1]])
    sum_l = x_sent(5, pair.at[1], at.to_left)
    own_l.wait_recv()
    sum_r.wait_recv()
    added(acc.at[pl.ds(0, half)], [half_of(x, 0), x_slots.at[3], x_slots.at[4]])
    own_r.wait_recv()
    sum_l.wait_recv()
    added(acc.at[pl.ds(half, half)], [half_of(x, 1), x_slots.at[2], x_slots.at[5]])

    def bit_at(at_y, at_z):
        return pl.ds(pl.multiple_of((at_y * 8 + at_z) * bit, bit), bit)

    arrive = []
    for i, (dz, dy) in enumerate(at.peers):
        at_y = 1 - y_hi if dy else y_hi
        src = acc.at[bit_at(at_y, lax.rem(z + dz, 8))]
        arrive.append(send(src, slots.at[i], rr, i, at.peer(dz, dy)))
    value = acc[bit_at(y_hi, z), :].astype(F32)
    for i, copy in enumerate(arrive):
        copy.wait_recv()
        value += slots[i].astype(F32)
    chunk[...] = (value / total).astype(BF16)

    piece = at.me
    mine = pl.ds(pl.multiple_of(x * block + (y_hi * 8 + z) * bit, bit), bit)
    arrive = []
    for i, (dz, dy) in enumerate(at.peers):
        arrive.append(send(chunk, gram.at[piece, mine], gr, i, at.peer(dz, dy)))
    gram[piece, mine] = chunk[...]
    for copy in arrive:
        copy.wait_recv()

    def at_half(which, owner, h):
        return gram.at[which, pl.ds(pl.multiple_of(owner * block + h * half, half), half)]

    def at_block(which, owner):
        return gram.at[which, span(owner, block)]

    def passed(src, sems, i, there):
        return send(src, src, sems, i, there)

    def to_y(i, owner):
        return (
            passed(at_half(piece, owner, 0), ys, 2 * i, at.near),
            passed(at_half(piece, owner, 1), ys, 2 * i + 1, at.far),
        )

    go_r = passed(at_block(piece, x), xg, 0, at.to_right)
    go_l = passed(at_block(piece, x), xg, 1, at.to_left)
    y_own = to_y(0, x)
    c_all = [passed(at_block(piece, x), cs, 0, at.sibling)]
    go_r.wait_recv()
    hop_r = passed(at_half(piece, left, 0), xg, 2, at.to_right)
    y_left = to_y(1, left)
    go_l.wait_recv()
    hop_l = passed(at_half(piece, right, 1), xg, 3, at.to_left)
    y_right = to_y(2, right)
    c_all.append(passed(at_block(piece, left), cs, 1, at.sibling))
    c_all.append(passed(at_block(piece, right), cs, 2, at.sibling))

    def from_y(copies, owner, i):
        for copy in copies:
            copy.wait_recv()
        c_all.append(passed(at_block(at.near_id, owner), cs, i, at.sibling))

    from_y(y_own, x, 3)
    hop_r.wait_recv()
    y_far = [passed(at_half(piece, across, 0), ys, 6, at.near)]
    hop_l.wait_recv()
    y_far.append(passed(at_half(piece, across, 1), ys, 7, at.far))
    c_all.append(passed(at_block(piece, across), cs, 4, at.sibling))
    from_y(y_left, left, 5)
    from_y(y_right, right, 6)
    from_y(y_far, across, 7)
    for copy in c_all:
        copy.wait_recv()


def white_steps(at, send, genes, gram, every, out, scratch):
    lower, start, first, second, leaving, os = scratch
    cols = every.shape[2]
    share = leaving.shape[1]
    pieces = 4
    tall = pieces * 2 * TILE

    def keep(dst, index, value):
        dst[span(index, TILE), :] = value
        dst[pl.ds(pl.multiple_of(tall + index * TILE, TILE), TILE), :] = value

    mine = span(at.me, share)
    for b in range(pieces):
        block = every[b, mine].astype(F32)
        block = jnp.concatenate([block, jnp.zeros((LANES - share, cols), F32)], axis=0)
        block = block.T.astype(BF16)
        for i in range(2):
            keep(start, 2 * b + i, block[i * TILE : (i + 1) * TILE])

    def strip(a, i, h):
        return gram[a, (i * 2 + h) * TILE : (i * 2 + h + 1) * TILE, :]

    spot = lax.broadcasted_iota(jnp.int32, (TILE, TILE), 0)
    spot = spot == lax.broadcasted_iota(jnp.int32, (TILE, TILE), 1)
    trace = F32(0)
    for a in range(pieces):
        for i in range(2):
            tile = strip(a, i, 0)[:, :TILE].astype(F32)
            trace += jnp.sum(jnp.where(spot, tile, F32(0)))
    scale = jnp.full((1, LANES), trace / genes + 1e-06, F32)
    inverse = 1.0 / scale
    rsqrt = 1.0 / jnp.sqrt(scale)

    @pl.loop(0, pieces)
    def _(a):
        for i in range(2):
            one, two, three = (lax.rem(2 * a + i + d, 8) for d in (1, 2, 3))
            flip = strip(a, i, 0)[:, TILE:].astype(F32).T.astype(BF16)
            lower[one, :, 2 * TILE :] = flip[:TILE]
            lower[two, : TILE // 2, TILE : 2 * TILE] = flip[TILE:]
            flip = strip(a, i, 1)[:, : WIDE - TILE].astype(F32).T.astype(BF16)
            lower[two, TILE // 2 :, TILE : 2 * TILE] = flip[: TILE // 2]
            lower[three, :, :TILE] = flip[TILE // 2 :]

    def image(left, a, i):
        j = 2 * a + i
        base = lax.rem(j + 5, 8) * TILE

        def rows(offset, size):
            return left[pl.ds(pl.multiple_of(base + offset, LANES), size), :]

        value = jnp.dot(lower[j], rows(0, 3 * TILE), preferred_element_type=F32)
        value += jnp.dot(strip(a, i, 0), rows(3 * TILE, WIDE), preferred_element_type=F32)
        value += jnp.dot(strip(a, i, 1), rows(3 * TILE + WIDE, WIDE), preferred_element_type=F32)
        return value * inverse

    def own(source, a, i):
        return source[span(2 * a + i, TILE), :].astype(F32)

    @pl.loop(0, pieces)
    def _(a):
        for i in range(2):
            keep(first, 2 * a + i, (1.5 * own(start, a, i) - 0.5 * image(start, a, i)).astype(BF16))

    @pl.loop(0, pieces)
    def _(a):
        for i in range(2):
            keep(second, 2 * a + i, image(first, a, i).astype(BF16))

    @pl.loop(0, pieces)
    def _(a):
        for i in range(2):
            inner = 1.5 * own(second, a, i) - 0.5 * image(second, a, i)
            keep(first, 2 * a + i, (1.5 * own(start, a, i) - 0.5 * inner).astype(BF16))

    coming = []
    targets = ((at.near_id, at.near), (at.cross_id, at.cross), (at.sib_id, at.sibling))
    for t, (a, there) in enumerate((*targets, (at.me, None))):
        for i in range(2):
            value = (1.5 * own(first, a, i) - 0.5 * image(first, a, i)) * rsqrt
            value = value.T[:share].astype(BF16)
            cols_at = slice(i * TILE, (i + 1) * TILE)
            if there is None:
                out[mine, cols_at] = value
            else:
                leaving[t, :, cols_at] = value
        if there is not None:
            coming.append(send(leaving.at[t], out.at[mine], os, t, there))
    for copy in coming:
        copy.wait_recv()


def kernel(sizes, total, dosage, pheno, perm, weight_rows, out, *scratch):
    refs, position = [], 0
    for size in sizes:
        refs.append(scratch[position : position + size])
        position += size
    plain, pairs, own_sem = refs
    pairs = [(pairs[i], pairs[i + 1]) for i in range(0, len(pairs), 2)]
    (
        coded, codes, placed, cols_in, turned, near_w, part, every,
        x_slots, pair, acc, slots, chunk, gram, lower, start, first, second, leaving,
    ) = plain
    at, send = Place(), Sender()
    barrier = pltpu.get_barrier_semaphore()
    greeted = [at.sibling, at.near, at.cross, at.far, at.far_cross, at.to_right, at.to_left]
    greeted += [at.peer(*p) for p in at.peers]
    for there in greeted:
        pl.semaphore_signal(barrier, inc=1, device_id=there, device_id_type=MESH)
    snps, own = dosage.shape
    mine = span(at.me, own)
    coded[:snps, mine] = dosage[...].astype(F32).astype(BF16)
    source = perm[...]
    both = jnp.concatenate([lax.shift_right_logical(source, 8), source & 255], axis=0)
    coded[snps:, mine] = both.astype(F32).astype(BF16)
    pl.semaphore_wait(barrier, len(greeted))
    score_steps(
        at, send, dosage, pheno, weight_rows, part, every,
        (coded, codes, placed, cols_in, turned, near_w, *pairs[:5], own_sem[0]),
    )
    spread_steps(at, send, total, part, gram, (x_slots, pair, acc, slots, chunk, *pairs[5:11]))
    white_steps(
        at, send, pheno.shape[1], gram, every, out,
        (lower, start, first, second, leaving, pairs[11]),
    )
    send.finish()


def shards(dosage, pheno, perm, snp_weight):
    snps, own = dosage.shape
    genes = pheno.shape[1]
    groups = lax.axis_size(SAMP)
    nulls = perm.shape[0]
    copies = nulls + 1
    rows = copies * snps
    cols = genes // groups
    samples = own * groups
    share = -(-rows // (16 * groups)) * 16
    tall = 4 * TILE
    weight_rows = jnp.tile(snp_weight, nulls)[:, None]
    dma = pltpu.SemaphoreType.DMA
    vmem = pl.BlockSpec(memory_space=pltpu.VMEM)
    plain = [
        pltpu.VMEM((snps + 2 * nulls, samples), BF16),
        pltpu.VMEM((2 * nulls, samples), F32),
        pltpu.VMEM((LEAD + rows, samples), BF16),
        pltpu.VMEM((samples, cols), BF16),
        pltpu.VMEM((cols, rows - snps), BF16),
        pltpu.VMEM((rows - snps, 3 * cols), BF16),
        pltpu.VMEM((tall, WIDE), BF16),
        pltpu.VMEM((groups, share * groups, cols), BF16),
        pltpu.VMEM((6, tall // 8, WIDE), BF16),
        pltpu.VMEM((2, tall // 8, WIDE), BF16),
        pltpu.VMEM((tall // 4, WIDE), BF16),
        pltpu.VMEM((15, tall // 64, WIDE), BF16),
        pltpu.VMEM((tall // 64, WIDE), BF16),
        pltpu.VMEM((groups, tall, WIDE), BF16),
        pltpu.VMEM((genes // TILE, TILE, 3 * TILE), BF16),
        *[pltpu.VMEM((2 * genes, LANES), BF16)] * 3,
        pltpu.VMEM((3, share, cols), BF16),
    ]
    counts = [3, 5, 3, 3, 3, 6, 15, 15, 4, 8, 8, 3]
    pairs = [dma((n,)) for n in counts for _ in range(2)]
    sizes = (len(plain), len(pairs), 1)
    white = pl.pallas_call(
        functools.partial(kernel, sizes, nulls * snps * lax.axis_size(SNP)),
        out_shape=jax.ShapeDtypeStruct((share * groups, cols), BF16),
        in_specs=[vmem, pl.BlockSpec(memory_space=pl.ANY), vmem, vmem],
        out_specs=vmem,
        scratch_shapes=[*plain, *pairs, dma],
        compiler_params=pltpu.CompilerParams(
            collective_id=0, has_side_effects=True, vmem_limit_bytes=48 << 20
        ),
        name="whitened_scores",
    )(dosage, pheno, perm, weight_rows)
    return white[:rows].reshape(copies, snps, cols)


def solution(mesh):
    finer = Mesh(mesh.devices.reshape(2, 2, 4, 8, 2), (*SAMP, *SNP))
    in_specs = (P(SNP, SAMP), P(SAMP, None), P(None, SAMP), P(SNP))
    return jax.shard_map(
        shards, mesh=finer, in_specs=in_specs, out_specs=P(None, SNP, SAMP), check_vma=False
    )
```

```python
import functools

import jax
import jax.numpy as jnp
from jax import lax
from jax.experimental import pallas as pl
from jax.experimental.pallas import tpu as pltpu
from jax.sharding import Mesh
from jax.sharding import PartitionSpec as P

SAMP = ("y_lo", "core")
SNP = ("x", "z", "y_hi")
F32 = jnp.float32
BF16 = jnp.bfloat16
NT = (((1,), (1,)), ((), ()))
LOW = 256
TILE = 256
LANES = 128
LEAD = 16
CHUNKS = 3
CUTS = ((0, 6), (6, 4))
MESH = pl.DeviceIdType.MESH


def span(index, size):
    return pl.ds(pl.multiple_of(index * size, size), size)


class Sender:
    def __init__(self):
        self.started = []

    def __call__(self, src, dst, sems, i, there):
        copy = pltpu.make_async_remote_copy(
            src_ref=src, dst_ref=dst, send_sem=sems[0].at[i], recv_sem=sems[1].at[i],
            device_id=there, device_id_type=MESH,
        )
        copy.start()
        self.started.append(copy)
        return copy

    def finish(self):
        for copy in self.started:
            copy.wait_send()


class Place:
    def __init__(self):
        x, z, y_hi = lax.axis_index("x"), lax.axis_index("z"), lax.axis_index("y_hi")
        y_lo, core = lax.axis_index("y_lo"), lax.axis_index("core")
        self.x, self.z, self.y_hi, self.y_lo, self.core = x, z, y_hi, y_lo, core
        self.me = y_lo * 2 + core
        self.sib_id = y_lo * 2 + 1 - core
        self.near_id = (1 - y_lo) * 2 + core
        self.cross_id = (1 - y_lo) * 2 + 1 - core
        self.sibling = {"core": 1 - core}
        self.near = {"y_lo": 1 - y_lo}
        self.cross = {"y_lo": 1 - y_lo, "core": 1 - core}
        self.far = {"y_lo": 1 - y_lo, "y_hi": 1 - y_hi}
        self.far_cross = {"y_lo": 1 - y_lo, "y_hi": 1 - y_hi, "core": 1 - core}
        self.right, self.left = lax.rem(x + 1, 4), lax.rem(x + 3, 4)
        self.across = lax.rem(x + 2, 4)
        self.to_right, self.to_left = {"x": self.right}, {"x": self.left}
        self.peers = [(dz, dy) for dz in range(8) for dy in range(2) if dz or dy]

    def peer(self, dz, dy):
        there = {"z": lax.rem(self.z + dz, 8)}
        if dy:
            there["y_hi"] = 1 - self.y_hi
        return there


def score_steps(at, send, dosage, pheno, snp_weight, part, every, scratch):
    coded, codes, placed, cols_in, turned, near_w, a, p, s, n, f, own_sem = scratch
    snps, own = dosage.shape
    samples, cols = cols_in.shape
    nulls = codes.shape[0] // 2
    copies = nulls + 1
    mine = span(at.me, own)
    coming = [
        send(coded.at[:, mine], coded.at[:, mine], a, i, there)
        for i, there in enumerate((at.near, at.cross, at.sibling))
    ]
    cut = own * 7 // 16
    pheno_coming = []
    for i, (there, target, first, size) in enumerate(
        (
            (at.near, at.near_id, 0, cut), (at.far, at.near_id, cut, own - cut),
            (at.cross, at.cross_id, 0, cut), (at.far_cross, at.cross_id, cut, own - cut),
        )
    ):
        pheno_coming.append(
            send(
                pheno.at[pl.ds(first, size), span(target, cols)],
                cols_in.at[pl.ds(pl.multiple_of(at.me * own + first, 32), size)],
                p, i, there,
            )
        )
    pheno_coming.append(
        send(pheno.at[:, span(at.sib_id, cols)], cols_in.at[mine], p, 4, at.sibling)
    )
    stay = pltpu.make_async_copy(pheno.at[:, span(at.me, cols)], cols_in.at[mine], own_sem)
    stay.start()
    placed[:LEAD, :] = jnp.ones((LEAD, samples), BF16)
    for owner in range(4):
        every[owner, copies * snps :] = jnp.zeros((every.shape[1] - copies * snps, cols), BF16)
    for copy in coming:
        copy.wait_recv()

    codes[...] = coded[snps:, :].astype(F32)
    dose = coded[:snps, :]
    placed[LEAD : LEAD + snps, :] = dose
    dose32 = dose.astype(F32)
    dose_mean = jnp.sum(dose32, axis=1, keepdims=True) / samples
    dose_square = jnp.sum(dose32 * dose32, axis=1, keepdims=True) / samples
    spread_rows = jnp.sqrt(samples * (dose_square + 1e-05))
    steps = samples // LOW

    @pl.loop(0, nulls)
    def _(k):
        high = codes[pl.ds(k, 1), :]
        low = codes[pl.ds(nulls + k, 1), :]
        values = coded[:snps, :]
        masked = jnp.concatenate(
            [values * (high == F32(h)).astype(F32).astype(BF16) for h in range(steps)], axis=0
        )
        ids = lax.broadcasted_iota(jnp.int32, (LOW, samples), 0).astype(F32)
        onehot = (ids == low).astype(F32).astype(BF16)
        got = lax.dot_general(masked, onehot, NT, preferred_element_type=F32).astype(BF16)
        rows = pl.ds(pl.multiple_of(LEAD + (k + 1) * snps, 16), snps)
        for h in range(steps):
            placed[rows, h * LOW : (h + 1) * LOW] = got[h * snps : (h + 1) * snps]

    stay.wait()
    for copy in pheno_coming:
        copy.wait_recv()

    per = copies // CHUNKS
    total = None
    to_sib, to_near = [], []
    for c in range(CHUNKS):
        first = 0 if c == 0 else LEAD + c * per * snps
        last = LEAD + (c + 1) * per * snps
        raw = jnp.dot(placed[first:last, :], cols_in[...], preferred_element_type=F32)
        if c == 0:
            total = raw[:1]
            raw = raw[LEAD:]
        for j in range(per):
            value = (raw[j * snps : (j + 1) * snps] - dose_mean * total) / spread_rows
            row = (c * per + j) * snps
            every[at.me, row : row + snps] = value.astype(BF16)
        block = every.at[at.me, pl.ds(c * per * snps, per * snps)]
        to_near.append(send(block, block, n, c, at.near))
        to_sib.append(send(block, block, s, c, at.sibling))

    end = copies * snps
    turned[...] = every[at.me, snps:end].astype(F32).T.astype(BF16)
    spot = lax.broadcasted_iota(jnp.int32, (snps, snps), 0)
    spot = spot == lax.broadcasted_iota(jnp.int32, (snps, snps), 1)
    weight = jnp.sum(jnp.where(spot, snp_weight[...], F32(0)), axis=1, keepdims=True)

    def weigh(r, which):
        for k in range(nulls):
            value = every[which, (k + 1) * snps : (k + 2) * snps].astype(F32) * weight
            near_w[k * snps : (k + 1) * snps, r * cols : (r + 1) * cols] = value.astype(BF16)

    def tile(row, i, first):
        got = jnp.dot(
            turned[i * TILE : (i + 1) * TILE, :],
            near_w[:, pl.ds(pl.multiple_of(first, TILE), TILE)], preferred_element_type=F32,
        )
        got = got.astype(BF16)
        for h in range(2):
            at_row = (2 * row + h) * TILE
            part[at_row : at_row + TILE, :] = got[:, h * LANES : (h + 1) * LANES]

    weigh(0, at.me)
    for copy in to_sib:
        copy.wait_recv()
    weigh(1, at.sib_id)
    for i in range(2):
        for t in range(2):
            tile(i * 3 + t, i, t * TILE)
        tile(i * 3 + 2, i, cols + lax.rem(i + at.core, 2) * TILE)
    yield
    passed = []

    def hand_on(c):
        to_near[c].wait_recv()
        block = every.at[at.near_id, pl.ds(c * per * snps, per * snps)]
        passed.append(send(block, block, f, c, at.sibling))

    hand_on(0)
    hand_on(1)
    yield
    hand_on(2)
    yield
    for copy in passed:
        copy.wait_recv()
    weigh(2, (1 - at.y_lo) * 2 + lax.rem(at.core + at.y_lo, 2))
    for i in range(2):
        for t in range(2):
            tile(6 + i * 2 + t, i, 2 * cols + t * TILE)
    yield


def spread_chunk(at, send, total, part, gram, scratch, k):
    x_slots, pair, acc, slots, chunk, xr, rr, gr, xg, ys, cs, own_in, own_out = scratch
    base, rows = (n * 2 * TILE for n in CUTS[k])
    block, half, bit = rows // 4, rows // 8, rows // 64
    x, z, y_hi = at.x, at.z, at.y_hi
    right, left, across = at.right, at.left, at.across
    x_slots, pair, acc = x_slots.at[k], pair.at[k], acc.at[k]
    slots, chunk = slots.at[k], chunk.at[k, pl.ds(0, bit)]

    def half_of(owner, h):
        return part.at[pl.ds(pl.multiple_of(base + owner * block + h * half, 64), half)]

    def slot(i):
        return x_slots.at[i, pl.ds(0, half)]

    def x_sent(i, src, there):
        return send(src, slot(i), xr, 6 * k + i, there)

    def added(dst, sources):
        @pl.loop(0, half, step=64)
        def _(r):
            rows_at = pl.ds(pl.multiple_of(r, 64), 64)
            value = sources[0][rows_at, :].astype(F32)
            for source in sources[1:]:
                value += source[rows_at, :].astype(F32)
            dst[rows_at, :] = value.astype(BF16)

    def summed(h):
        return pair.at[h, pl.ds(0, half)]

    hop_r = x_sent(0, half_of(across, 0), at.to_right)
    hop_l = x_sent(1, half_of(across, 1), at.to_left)
    own_r = x_sent(2, half_of(right, 1), at.to_right)
    own_l = x_sent(3, half_of(left, 0), at.to_left)
    yield
    hop_r.wait_recv()
    added(summed(0), [half_of(right, 0), slot(0)])
    sum_r = x_sent(4, summed(0), at.to_right)
    hop_l.wait_recv()
    added(summed(1), [half_of(left, 1), slot(1)])
    sum_l = x_sent(5, summed(1), at.to_left)
    yield
    own_l.wait_recv()
    sum_r.wait_recv()
    added(acc.at[pl.ds(0, half)], [half_of(x, 0), slot(3), slot(4)])
    own_r.wait_recv()
    sum_l.wait_recv()
    added(acc.at[pl.ds(half, half)], [half_of(x, 1), slot(2), slot(5)])

    def bit_at(at_y, at_z):
        return acc.at[pl.ds(pl.multiple_of((at_y * 8 + at_z) * bit, 16), bit)]

    arrive = []
    for i, (dz, dy) in enumerate(at.peers):
        at_y = 1 - y_hi if dy else y_hi
        src = bit_at(at_y, lax.rem(z + dz, 8))
        dst = slots.at[i, pl.ds(0, bit)]
        arrive.append(send(src, dst, rr, 15 * k + i, at.peer(dz, dy)))
    stay = pltpu.make_async_copy(bit_at(y_hi, z), slots.at[15, pl.ds(0, bit)], own_in.at[k])
    stay.start()
    yield
    stay.wait()
    value = slots[15, :bit].astype(F32)
    for i, copy in enumerate(arrive):
        copy.wait_recv()
        value += slots[i, :bit].astype(F32)
    chunk[...] = (value / total).astype(BF16)

    piece = at.me
    first = base + x * block + (y_hi * 8 + z) * bit
    dst = gram.at[piece, pl.ds(pl.multiple_of(first, 16), bit)]
    arrive = []
    for i, (dz, dy) in enumerate(at.peers):
        arrive.append(send(chunk, dst, gr, 15 * k + i, at.peer(dz, dy)))
    stay = pltpu.make_async_copy(chunk, dst, own_out.at[k])
    stay.start()
    yield
    stay.wait()
    for copy in arrive:
        copy.wait_recv()

    def at_half(which, owner, h):
        return gram.at[which, pl.ds(pl.multiple_of(base + owner * block + h * half, 64), half)]

    def at_block(which, owner):
        return gram.at[which, pl.ds(pl.multiple_of(base + owner * block, 128), block)]

    def to_x(i, src, there):
        return send(src, src, xg, 4 * k + i, there)

    c_all = []

    def to_sibling(which, owner):
        src = at_block(which, owner)
        c_all.append(send(src, src, cs, 8 * k + len(c_all), at.sibling))

    def to_y(i, owner, h):
        src = at_half(piece, owner, h)
        return send(src, src, ys, 8 * k + 2 * i + h, at.far if h else at.near)

    go_r = to_x(0, at_block(piece, x), at.to_right)
    go_l = to_x(1, at_block(piece, x), at.to_left)
    y_own = [to_y(0, x, h) for h in range(2)]
    to_sibling(piece, x)
    yield
    go_r.wait_recv()
    hop_r = to_x(2, at_half(piece, left, 0), at.to_right)
    y_left = [to_y(1, left, h) for h in range(2)]
    go_l.wait_recv()
    hop_l = to_x(3, at_half(piece, right, 1), at.to_left)
    y_right = [to_y(2, right, h) for h in range(2)]
    to_sibling(piece, left)
    to_sibling(piece, right)

    def from_y(copies, owner):
        for copy in copies:
            copy.wait_recv()
        to_sibling(at.near_id, owner)

    yield
    hop_r.wait_recv()
    y_far = [to_y(3, across, 0)]
    hop_l.wait_recv()
    y_far.append(to_y(3, across, 1))
    to_sibling(piece, across)
    from_y(y_own, x)
    yield
    from_y(y_left, left)
    from_y(y_right, right)
    yield
    from_y(y_far, across)
    yield
    for copy in c_all:
        copy.wait_recv()


def white_steps(at, send, genes, gram, every, out, scratch):
    lower, start, first, second, partial, leaving, os = scratch
    cols = every.shape[2]
    share = leaving.shape[1]
    pieces = 4

    mine = span(at.me, share)
    for b in range(pieces):
        block = every[b, mine].astype(F32)
        block = jnp.concatenate([block, jnp.zeros((LANES - share, cols), F32)], axis=0)
        start[b * cols : (b + 1) * cols, :] = block.T.astype(BF16)
    yield

    def strip(a, row):
        first, last = 2 * row * TILE, 2 * (row + 1) * TILE
        halves = gram[a, first : first + TILE, :], gram[a, first + TILE : last, :]
        return jnp.concatenate(halves, axis=1)

    def flipped(a, row):
        return strip(a, row).astype(F32).T.astype(BF16)

    def product(tile, left, j):
        return jnp.dot(tile, left[span(j, TILE), :], preferred_element_type=F32)

    def places(a, i):
        c, y = lax.rem(a, 2), a // 2
        pair = 2 * (2 * y + 1 - c) + lax.rem(i + c, 2)
        rest = 2 * (2 * y + 1 - c) + 1 - lax.rem(i + c, 2)
        direct = 2 * (1 - y) + lax.rem(c + y, 2)
        turned = 2 * (1 - y) + 1 - lax.rem(c + y, 2)
        return pair, rest, direct, turned

    spot = lax.broadcasted_iota(jnp.int32, (TILE, TILE), 0)
    spot = spot == lax.broadcasted_iota(jnp.int32, (TILE, TILE), 1)
    trace = F32(0)
    for a in range(pieces):
        for i in range(2):
            trace += jnp.sum(jnp.where(spot, strip(a, i * 3 + i).astype(F32), F32(0)))
    scale = jnp.full((1, LANES), trace / genes + 1e-06, F32)
    inverse = 1.0 / scale
    rsqrt = 1.0 / jnp.sqrt(scale)

    @pl.loop(0, pieces)
    def _(a):
        for i in range(2):
            lower[places(a, i)[0], :, :TILE] = flipped(a, i * 3 + 2)

    def on_chip(left, a, i):
        pair, rest, _, _ = places(a, i)
        value = product(strip(a, i * 3), left, 2 * a)
        value += product(strip(a, i * 3 + 1), left, 2 * a + 1)
        value += product(strip(a, i * 3 + 2), left, pair)
        return value + product(lower[2 * a + i, :, :TILE], left, rest)

    def off_chip(left, a, i):
        _, _, direct, turned = places(a, i)
        value = None
        for t in range(2):
            one = product(strip(a, 6 + i * 2 + t), left, 2 * direct + t)
            one += product(lower[2 * a + i, :, (t + 1) * TILE : (t + 2) * TILE], left, 2 * turned + t)
            value = one if value is None else value + one
        return value

    def image(left, a, i):
        return (on_chip(left, a, i) + off_chip(left, a, i)) * inverse

    def own(source, a, i):
        return source[span(2 * a + i, TILE), :].astype(F32)

    @pl.loop(0, pieces)
    def _(a):
        for i in range(2):
            partial[span(2 * a + i, TILE), :] = on_chip(start, a, i)

    yield

    @pl.loop(0, pieces)
    def _(a):
        for i in range(2):
            direct = places(a, i)[2]
            for t in range(2):
                lower[2 * direct + t, :, (i + 1) * TILE : (i + 2) * TILE] = flipped(a, 6 + i * 2 + t)

    @pl.loop(0, pieces)
    def _(a):
        for i in range(2):
            value = (partial[span(2 * a + i, TILE), :] + off_chip(start, a, i)) * inverse
            first[span(2 * a + i, TILE), :] = (1.5 * own(start, a, i) - 0.5 * value).astype(BF16)

    @pl.loop(0, pieces)
    def _(a):
        for i in range(2):
            second[span(2 * a + i, TILE), :] = image(first, a, i).astype(BF16)

    @pl.loop(0, pieces)
    def _(a):
        for i in range(2):
            inner = 1.5 * own(second, a, i) - 0.5 * image(second, a, i)
            first[span(2 * a + i, TILE), :] = (1.5 * own(start, a, i) - 0.5 * inner).astype(BF16)

    coming = []
    targets = ((at.near_id, at.near), (at.cross_id, at.cross), (at.sib_id, at.sibling))
    for t, (a, there) in enumerate((*targets, (at.me, None))):
        for i in range(2):
            value = (1.5 * own(first, a, i) - 0.5 * image(first, a, i)) * rsqrt
            value = value.T[:share].astype(BF16)
            cols_at = slice(i * TILE, (i + 1) * TILE)
            if there is None:
                out[mine, cols_at] = value
            else:
                leaving[t, :, cols_at] = value
        if there is not None:
            coming.append(send(leaving.at[t], out.at[mine], os, t, there))
    for copy in coming:
        copy.wait_recv()
    yield


def kernel(sizes, total, dosage, pheno, perm, snp_weight, out, *scratch):
    refs, position = [], 0
    for size in sizes:
        refs.append(scratch[position : position + size])
        position += size
    plain, pairs, (singles,) = refs
    pairs = [(pairs[i], pairs[i + 1]) for i in range(0, len(pairs), 2)]
    (
        coded, codes, placed, cols_in, turned, near_w, part, every,
        x_slots, pair, acc, slots, chunk, gram, lower, start, first, second, partial, leaving,
        dose_here, perm_here,
    ) = plain
    at, send = Place(), Sender()
    barrier = pltpu.get_barrier_semaphore()
    greeted = [at.sibling, at.near, at.cross, at.far, at.far_cross, at.to_right, at.to_left]
    greeted += [at.peer(*p) for p in at.peers]
    for there in greeted:
        pl.semaphore_signal(barrier, inc=1, device_id=there, device_id_type=MESH)
    snps, own = dosage.shape
    mine = span(at.me, own)
    loads = [
        pltpu.make_async_copy(dosage, dose_here, singles.at[1]),
        pltpu.make_async_copy(perm, perm_here, singles.at[2]),
    ]
    for load in loads:
        load.start()
    for load in loads:
        load.wait()
    coded[:snps, mine] = dose_here[...].astype(F32).astype(BF16)
    source = perm_here[...]
    both = jnp.concatenate([lax.shift_right_logical(source, 8), source & 255], axis=0)
    coded[snps:, mine] = both.astype(F32).astype(BF16)
    pl.semaphore_wait(barrier, len(greeted))
    scores = score_steps(
        at, send, dosage, pheno, snp_weight, part, every,
        (coded, codes, placed, cols_in, turned, near_w, *pairs[:5], singles.at[0]),
    )
    moved = (
        x_slots, pair, acc, slots, chunk, *pairs[5:11], singles.at[pl.ds(3, 2)], singles.at[pl.ds(5, 2)],
    )
    here, cross = (spread_chunk(at, send, total, part, gram, moved, k) for k in range(2))
    white = white_steps(
        at, send, pheno.shape[1], gram, every, out,
        (lower, start, first, second, partial, leaving, pairs[11]),
    )
    for _ in range(3):
        next(scores)
        next(here)
    next(scores)
    next(cross)
    next(white)
    for _ in here:
        next(cross)
    next(white)
    for _ in cross:
        pass
    next(white)
    send.finish()


def shards(dosage, pheno, perm, snp_weight):
    snps, own = dosage.shape
    genes = pheno.shape[1]
    groups = lax.axis_size(SAMP)
    nulls = perm.shape[0]
    copies = nulls + 1
    rows = copies * snps
    cols = genes // groups
    samples = own * groups
    share = -(-rows // (16 * groups)) * 16
    tiles = 10
    most = max(n for _, n in CUTS) * 2 * TILE
    dma = pltpu.SemaphoreType.DMA
    vmem = pl.BlockSpec(memory_space=pltpu.VMEM)
    hbm = pl.BlockSpec(memory_space=pltpu.HBM)
    plain = [
        pltpu.VMEM((snps + 2 * nulls, samples), BF16),
        pltpu.VMEM((2 * nulls, samples), F32),
        pltpu.VMEM((LEAD + rows, samples), BF16),
        pltpu.VMEM((samples, cols), BF16),
        pltpu.VMEM((cols, rows - snps), BF16),
        pltpu.VMEM((rows - snps, 3 * cols), BF16),
        pltpu.VMEM((tiles * 2 * TILE, LANES), BF16),
        pltpu.VMEM((groups, share * groups, cols), BF16),
        pltpu.VMEM((2, 6, most // 8, LANES), BF16),
        pltpu.VMEM((2, 2, most // 8, LANES), BF16),
        pltpu.VMEM((2, most // 4, LANES), BF16),
        pltpu.VMEM((2, 16, most // 64, LANES), BF16),
        pltpu.VMEM((2, most // 64, LANES), BF16),
        pltpu.VMEM((groups, tiles * 2 * TILE, LANES), BF16),
        pltpu.VMEM((genes // TILE, TILE, 3 * TILE), BF16),
        *[pltpu.VMEM((genes, LANES), BF16)] * 3,
        pltpu.VMEM((genes, LANES), F32),
        pltpu.VMEM((3, share, cols), BF16),
        pltpu.VMEM(dosage.shape, jnp.int32),
        pltpu.VMEM(perm.shape, jnp.int32),
    ]
    each = len(CUTS)
    counts = [3, 5, 3, 3, 3, *[n * each for n in (6, 15, 15, 4, 8, 8)], 3]
    pairs = [dma((n,)) for n in counts for _ in range(2)]
    sizes = (len(plain), len(pairs), 1)
    white = pl.pallas_call(
        functools.partial(kernel, sizes, nulls * snps * lax.axis_size(SNP)),
        out_shape=jax.ShapeDtypeStruct((share * groups, cols), BF16),
        in_specs=[hbm, hbm, hbm, vmem],
        out_specs=vmem,
        scratch_shapes=[*plain, *pairs, dma((7,))],
        compiler_params=pltpu.CompilerParams(
            collective_id=0, has_side_effects=True, vmem_limit_bytes=60 << 20
        ),
        name="whitened_scores",
    )(dosage, pheno, perm, snp_weight[None, :])
    return white[:rows].reshape(copies, snps, cols)


def solution(mesh):
    finer = Mesh(mesh.devices.reshape(2, 2, 4, 8, 2), (*SAMP, *SNP))
    in_specs = (P(SNP, SAMP), P(SAMP, None), P(None, SAMP), P(SNP))
    return jax.shard_map(
        shards, mesh=finer, in_specs=in_specs, out_specs=P(None, SNP, SAMP), check_vma=False
    )
```

```python
import functools

import jax
import jax.numpy as jnp
from jax import lax
from jax.experimental import pallas as pl
from jax.experimental.pallas import tpu as pltpu
from jax.sharding import Mesh
from jax.sharding import PartitionSpec as P

SAMP = ("y_lo", "core")
SNP = ("x", "z", "y_hi")
F32 = jnp.float32
BF16 = jnp.bfloat16
NT = (((1,), (1,)), ((), ()))
LOW = 256
TILE = 256
LANES = 128
LEAD = 16
CHUNKS = 3
CUTS = ((0, 6), (6, 4))
MESH = pl.DeviceIdType.MESH


def span(index, size):
    return pl.ds(pl.multiple_of(index * size, size), size)


class Sender:
    def __init__(self):
        self.started, self.older = [], []

    def __call__(self, src, dst, sems, i, there):
        copy = pltpu.make_async_remote_copy(
            src_ref=src, dst_ref=dst, send_sem=sems[0].at[i], recv_sem=sems[1].at[i],
            device_id=there, device_id_type=MESH,
        )
        copy.start()
        self.started.append(copy)
        return copy

    def settle(self):
        for copy in self.older:
            copy.wait_send()
        self.started, self.older = [], self.started

    def finish(self):
        for copy in self.older + self.started:
            copy.wait_send()


class Place:
    def __init__(self):
        x, z, y_hi = lax.axis_index("x"), lax.axis_index("z"), lax.axis_index("y_hi")
        y_lo, core = lax.axis_index("y_lo"), lax.axis_index("core")
        self.x, self.z, self.y_hi, self.y_lo, self.core = x, z, y_hi, y_lo, core
        self.me = y_lo * 2 + core
        self.sib_id = y_lo * 2 + 1 - core
        self.near_id = (1 - y_lo) * 2 + core
        self.cross_id = (1 - y_lo) * 2 + 1 - core
        self.sibling = {"core": 1 - core}
        self.near = {"y_lo": 1 - y_lo}
        self.cross = {"y_lo": 1 - y_lo, "core": 1 - core}
        self.far = {"y_lo": 1 - y_lo, "y_hi": 1 - y_hi}
        self.far_cross = {"y_lo": 1 - y_lo, "y_hi": 1 - y_hi, "core": 1 - core}
        self.right, self.left = lax.rem(x + 1, 4), lax.rem(x + 3, 4)
        self.across = lax.rem(x + 2, 4)
        self.to_right, self.to_left = {"x": self.right}, {"x": self.left}
        self.peers = [(dz, dy) for dz in range(8) for dy in range(2) if dz or dy]

    def peer(self, dz, dy):
        there = {"z": lax.rem(self.z + dz, 8)}
        if dy:
            there["y_hi"] = 1 - self.y_hi
        return there


def score_steps(at, send, dosage, pheno, snp_weight, part, every, scratch):
    coded, codes, placed, cols_in, turned, near_w, a, p, s, n, f, own_sem = scratch
    snps, own = dosage.shape
    samples, cols = cols_in.shape
    nulls = codes.shape[0] // 2
    copies = nulls + 1
    mine = span(at.me, own)
    coming = [
        send(coded.at[:, mine], coded.at[:, mine], a, i, there)
        for i, there in enumerate((at.near, at.cross, at.sibling))
    ]
    cut = own * 7 // 16
    pheno_coming = []
    for i, (there, target, first, size) in enumerate(
        (
            (at.near, at.near_id, 0, cut), (at.far, at.near_id, cut, own - cut),
            (at.cross, at.cross_id, 0, cut), (at.far_cross, at.cross_id, cut, own - cut),
        )
    ):
        pheno_coming.append(
            send(
                pheno.at[pl.ds(first, size), span(target, cols)],
                cols_in.at[pl.ds(pl.multiple_of(at.me * own + first, 32), size)],
                p, i, there,
            )
        )
    pheno_coming.append(
        send(pheno.at[:, span(at.sib_id, cols)], cols_in.at[mine], p, 4, at.sibling)
    )
    stay = pltpu.make_async_copy(pheno.at[:, span(at.me, cols)], cols_in.at[mine], own_sem)
    stay.start()
    placed[:LEAD, :] = jnp.ones((LEAD, samples), BF16)
    for owner in range(4):
        every[owner, copies * snps :] = jnp.zeros((every.shape[1] - copies * snps, cols), BF16)
    for copy in coming:
        copy.wait_recv()

    codes[...] = coded[snps:, :].astype(F32)
    dose = coded[:snps, :]
    placed[LEAD : LEAD + snps, :] = dose
    dose32 = dose.astype(F32)
    dose_mean = jnp.sum(dose32, axis=1, keepdims=True) / samples
    dose_square = jnp.sum(dose32 * dose32, axis=1, keepdims=True) / samples
    spread_rows = jnp.sqrt(samples * (dose_square + 1e-05))
    steps = samples // LOW

    @pl.loop(0, nulls)
    def _(k):
        high = codes[pl.ds(k, 1), :]
        low = codes[pl.ds(nulls + k, 1), :]
        values = coded[:snps, :]
        masked = jnp.concatenate(
            [values * (high == F32(h)).astype(F32).astype(BF16) for h in range(steps)], axis=0
        )
        ids = lax.broadcasted_iota(jnp.int32, (LOW, samples), 0).astype(F32)
        onehot = (ids == low).astype(F32).astype(BF16)
        got = lax.dot_general(masked, onehot, NT, preferred_element_type=F32).astype(BF16)
        rows = pl.ds(pl.multiple_of(LEAD + (k + 1) * snps, 16), snps)
        for h in range(steps):
            placed[rows, h * LOW : (h + 1) * LOW] = got[h * snps : (h + 1) * snps]

    stay.wait()
    for copy in pheno_coming:
        copy.wait_recv()

    per = copies // CHUNKS
    total = None
    to_sib, to_near = [], []
    for c in range(CHUNKS):
        first = 0 if c == 0 else LEAD + c * per * snps
        last = LEAD + (c + 1) * per * snps
        raw = jnp.dot(placed[first:last, :], cols_in[...], preferred_element_type=F32)
        if c == 0:
            total = raw[:1]
            raw = raw[LEAD:]
        for j in range(per):
            value = (raw[j * snps : (j + 1) * snps] - dose_mean * total) / spread_rows
            row = (c * per + j) * snps
            every[at.me, row : row + snps] = value.astype(BF16)
        block = every.at[at.me, pl.ds(c * per * snps, per * snps)]
        to_near.append(send(block, block, n, c, at.near))
        to_sib.append(send(block, block, s, c, at.sibling))

    end = copies * snps
    turned[...] = every[at.me, snps:end].astype(F32).T.astype(BF16)
    spot = lax.broadcasted_iota(jnp.int32, (snps, snps), 0)
    spot = spot == lax.broadcasted_iota(jnp.int32, (snps, snps), 1)
    weight = jnp.sum(jnp.where(spot, snp_weight[...], F32(0)), axis=1, keepdims=True)

    def weigh(r, which):
        for k in range(nulls):
            value = every[which, (k + 1) * snps : (k + 2) * snps].astype(F32) * weight
            near_w[k * snps : (k + 1) * snps, r * cols : (r + 1) * cols] = value.astype(BF16)

    def tile(row, i, first):
        got = jnp.dot(
            turned[i * TILE : (i + 1) * TILE, :],
            near_w[:, pl.ds(pl.multiple_of(first, TILE), TILE)], preferred_element_type=F32,
        )
        got = got.astype(BF16)
        for h in range(2):
            at_row = (2 * row + h) * TILE
            part[at_row : at_row + TILE, :] = got[:, h * LANES : (h + 1) * LANES]

    weigh(0, at.me)
    for copy in to_sib:
        copy.wait_recv()
    weigh(1, at.sib_id)
    for i in range(2):
        for t in range(2):
            tile(i * 3 + t, i, t * TILE)
        tile(i * 3 + 2, i, cols + lax.rem(i + at.core, 2) * TILE)
    yield
    passed = []

    def hand_on(c):
        to_near[c].wait_recv()
        block = every.at[at.near_id, pl.ds(c * per * snps, per * snps)]
        passed.append(send(block, block, f, c, at.sibling))

    hand_on(0)
    hand_on(1)
    yield
    hand_on(2)
    yield
    for copy in passed:
        copy.wait_recv()
    weigh(2, (1 - at.y_lo) * 2 + lax.rem(at.core + at.y_lo, 2))
    for i in range(2):
        for t in range(2):
            tile(6 + i * 2 + t, i, 2 * cols + t * TILE)
    yield


def spread_chunk(at, send, total, part, gram, scratch, k):
    x_slots, acc, slots, chunk, xr, rr, gr, xg, ys, cs, own_in, own_out = scratch
    base, rows = (n * 2 * TILE for n in CUTS[k])
    block, half, bit = rows // 4, rows // 8, rows // 64
    x, z, y_hi = at.x, at.z, at.y_hi
    right, left, across = at.right, at.left, at.across
    x_slots, acc = x_slots.at[k], acc.at[k]
    slots, chunk = slots.at[k], chunk.at[k, pl.ds(0, bit)]

    def slot(i):
        return x_slots.at[i, pl.ds(0, block)]

    def x_sent(i, src, there):
        return send(src, slot(i), xr, 3 * k + i, there)

    def added(dst, sources):
        @pl.loop(0, block, step=64)
        def _(r):
            rows_at = pl.ds(pl.multiple_of(r, 64), 64)
            value = sources[0][rows_at, :].astype(F32)
            for source in sources[1:]:
                value += source[rows_at, :].astype(F32)
            dst[rows_at, :] = value.astype(BF16)

    def block_of(owner):
        return part.at[pl.ds(pl.multiple_of(base + owner * block, 128), block)]

    across_way = {"x": across}
    arrive = [
        x_sent(i, block_of(owner), there)
        for i, (owner, there) in enumerate(
            ((across, across_way), (right, at.to_right), (left, at.to_left))
        )
    ]
    yield
    for copy in arrive:
        copy.wait_recv()
    added(acc.at[pl.ds(0, block)], [block_of(x), slot(0), slot(1), slot(2)])

    def bit_at(at_y, at_z):
        return acc.at[pl.ds(pl.multiple_of((at_y * 8 + at_z) * bit, 16), bit)]

    arrive = []
    for i, (dz, dy) in enumerate(at.peers):
        at_y = 1 - y_hi if dy else y_hi
        src = bit_at(at_y, lax.rem(z + dz, 8))
        dst = slots.at[i, pl.ds(0, bit)]
        arrive.append(send(src, dst, rr, 15 * k + i, at.peer(dz, dy)))
    stay = pltpu.make_async_copy(bit_at(y_hi, z), slots.at[15, pl.ds(0, bit)], own_in.at[k])
    stay.start()
    yield
    stay.wait()
    value = slots[15, :bit].astype(F32)
    for i, copy in enumerate(arrive):
        copy.wait_recv()
        value += slots[i, :bit].astype(F32)
    chunk[...] = (value / total).astype(BF16)

    piece = at.me
    first = base + x * block + (y_hi * 8 + z) * bit
    dst = gram.at[piece, pl.ds(pl.multiple_of(first, 16), bit)]
    arrive = []
    for i, (dz, dy) in enumerate(at.peers):
        arrive.append(send(chunk, dst, gr, 15 * k + i, at.peer(dz, dy)))
    stay = pltpu.make_async_copy(chunk, dst, own_out.at[k])
    stay.start()
    yield
    stay.wait()
    for copy in arrive:
        copy.wait_recv()

    def at_half(which, owner, h):
        return gram.at[which, pl.ds(pl.multiple_of(base + owner * block + h * half, 64), half)]

    def at_block(which, owner):
        return gram.at[which, pl.ds(pl.multiple_of(base + owner * block, 128), block)]

    def to_x(i, src, there):
        return send(src, src, xg, 3 * k + i, there)

    c_all = []

    def to_sibling(which, owner):
        src = at_block(which, owner)
        c_all.append(send(src, src, cs, 8 * k + len(c_all), at.sibling))

    def to_y(i, owner, h):
        src = at_half(piece, owner, h)
        return send(src, src, ys, 8 * k + 2 * i + h, at.far if h else at.near)

    def from_y(copies, owner):
        for copy in copies:
            copy.wait_recv()
        to_sibling(at.near_id, owner)

    ways = ((at.to_right, left), (at.to_left, right), (across_way, across))
    x_coming = [to_x(i, at_block(piece, x), there) for i, (there, _) in enumerate(ways)]
    y_own = [to_y(0, x, h) for h in range(2)]
    to_sibling(piece, x)
    yield
    y_coming = []
    for i, (copy, (_, owner)) in enumerate(zip(x_coming, ways)):
        copy.wait_recv()
        y_coming.append([to_y(i + 1, owner, h) for h in range(2)])
        to_sibling(piece, owner)
    from_y(y_own, x)
    yield
    for copies, (_, owner) in zip(y_coming, ways):
        from_y(copies, owner)
    yield
    for copy in c_all:
        copy.wait_recv()


def white_steps(at, send, genes, gram, every, out, scratch):
    lower, start, first, second, partial, leaving, os = scratch
    cols = every.shape[2]
    share = leaving.shape[1]
    pieces = 4

    mine = span(at.me, share)
    for b in range(pieces):
        block = every[b, mine].astype(F32)
        block = jnp.concatenate([block, jnp.zeros((LANES - share, cols), F32)], axis=0)
        start[b * cols : (b + 1) * cols, :] = block.T.astype(BF16)
    yield

    def strip(a, row):
        first, last = 2 * row * TILE, 2 * (row + 1) * TILE
        halves = gram[a, first : first + TILE, :], gram[a, first + TILE : last, :]
        return jnp.concatenate(halves, axis=1)

    def flipped(a, row):
        return strip(a, row).astype(F32).T.astype(BF16)

    def product(tile, left, j):
        return jnp.dot(tile, left[span(j, TILE), :], preferred_element_type=F32)

    def places(a, i):
        c, y = lax.rem(a, 2), a // 2
        pair = 2 * (2 * y + 1 - c) + lax.rem(i + c, 2)
        rest = 2 * (2 * y + 1 - c) + 1 - lax.rem(i + c, 2)
        direct = 2 * (1 - y) + lax.rem(c + y, 2)
        turned = 2 * (1 - y) + 1 - lax.rem(c + y, 2)
        return pair, rest, direct, turned

    spot = lax.broadcasted_iota(jnp.int32, (TILE, TILE), 0)
    spot = spot == lax.broadcasted_iota(jnp.int32, (TILE, TILE), 1)
    trace = F32(0)
    for a in range(pieces):
        for i in range(2):
            trace += jnp.sum(jnp.where(spot, strip(a, i * 3 + i).astype(F32), F32(0)))
    scale = jnp.full((1, LANES), trace / genes + 1e-06, F32)
    inverse = 1.0 / scale
    rsqrt = 1.0 / jnp.sqrt(scale)

    @pl.loop(0, pieces)
    def _(a):
        for i in range(2):
            lower[places(a, i)[0], :, :TILE] = flipped(a, i * 3 + 2)

    def on_chip(left, a, i):
        pair, rest, _, _ = places(a, i)
        value = product(strip(a, i * 3), left, 2 * a)
        value += product(strip(a, i * 3 + 1), left, 2 * a + 1)
        value += product(strip(a, i * 3 + 2), left, pair)
        return value + product(lower[2 * a + i, :, :TILE], left, rest)

    def off_chip(left, a, i):
        _, _, direct, turned = places(a, i)
        value = None
        for t in range(2):
            one = product(strip(a, 6 + i * 2 + t), left, 2 * direct + t)
            one += product(lower[2 * a + i, :, (t + 1) * TILE : (t + 2) * TILE], left, 2 * turned + t)
            value = one if value is None else value + one
        return value

    def image(left, a, i):
        return (on_chip(left, a, i) + off_chip(left, a, i)) * inverse

    def own(source, a, i):
        return source[span(2 * a + i, TILE), :].astype(F32)

    @pl.loop(0, pieces)
    def _(a):
        for i in range(2):
            partial[span(2 * a + i, TILE), :] = on_chip(start, a, i)

    yield

    @pl.loop(0, pieces)
    def _(a):
        for i in range(2):
            direct = places(a, i)[2]
            for t in range(2):
                lower[2 * direct + t, :, (i + 1) * TILE : (i + 2) * TILE] = flipped(a, 6 + i * 2 + t)

    @pl.loop(0, pieces)
    def _(a):
        for i in range(2):
            value = (partial[span(2 * a + i, TILE), :] + off_chip(start, a, i)) * inverse
            first[span(2 * a + i, TILE), :] = (1.5 * own(start, a, i) - 0.5 * value).astype(BF16)

    @pl.loop(0, pieces)
    def _(a):
        for i in range(2):
            second[span(2 * a + i, TILE), :] = image(first, a, i).astype(BF16)

    @pl.loop(0, pieces)
    def _(a):
        for i in range(2):
            inner = 1.5 * own(second, a, i) - 0.5 * image(second, a, i)
            first[span(2 * a + i, TILE), :] = (1.5 * own(start, a, i) - 0.5 * inner).astype(BF16)

    coming = []
    targets = ((at.near_id, at.near), (at.cross_id, at.cross), (at.sib_id, at.sibling))
    for t, (a, there) in enumerate((*targets, (at.me, None))):
        for i in range(2):
            value = (1.5 * own(first, a, i) - 0.5 * image(first, a, i)) * rsqrt
            value = value.T[:share].astype(BF16)
            cols_at = slice(i * TILE, (i + 1) * TILE)
            if there is None:
                out[mine, cols_at] = value
            else:
                leaving[t, :, cols_at] = value
        if there is not None:
            coming.append(send(leaving.at[t], out.at[mine], os, t, there))
    send.settle()
    for copy in coming:
        copy.wait_recv()
    yield


def kernel(sizes, total, dosage, pheno, perm, snp_weight, out, *scratch):
    refs, position = [], 0
    for size in sizes:
        refs.append(scratch[position : position + size])
        position += size
    plain, pairs, (singles,) = refs
    pairs = [(pairs[i], pairs[i + 1]) for i in range(0, len(pairs), 2)]
    (
        coded, codes, placed, cols_in, turned, near_w, part, every,
        x_slots, acc, slots, chunk, gram, lower, start, first, second, partial, leaving,
        dose_here, perm_here,
    ) = plain
    at, send = Place(), Sender()
    barrier = pltpu.get_barrier_semaphore()
    greeted = [at.sibling, at.near, at.cross, at.far, at.far_cross]
    greeted += [at.to_right, at.to_left, {"x": at.across}]
    greeted += [at.peer(*p) for p in at.peers]
    for there in greeted:
        pl.semaphore_signal(barrier, inc=1, device_id=there, device_id_type=MESH)
    snps, own = dosage.shape
    mine = span(at.me, own)
    loads = [
        pltpu.make_async_copy(dosage, dose_here, singles.at[1]),
        pltpu.make_async_copy(perm, perm_here, singles.at[2]),
    ]
    for load in loads:
        load.start()
    for load in loads:
        load.wait()
    coded[:snps, mine] = dose_here[...].astype(F32).astype(BF16)
    source = perm_here[...]
    both = jnp.concatenate([lax.shift_right_logical(source, 8), source & 255], axis=0)
    coded[snps:, mine] = both.astype(F32).astype(BF16)
    pl.semaphore_wait(barrier, len(greeted))
    scores = score_steps(
        at, send, dosage, pheno, snp_weight, part, every,
        (coded, codes, placed, cols_in, turned, near_w, *pairs[:5], singles.at[0]),
    )
    moved = (
        x_slots, acc, slots, chunk, *pairs[5:11], singles.at[pl.ds(3, 2)], singles.at[pl.ds(5, 2)],
    )
    here, cross = (spread_chunk(at, send, total, part, gram, moved, k) for k in range(2))
    white = white_steps(
        at, send, pheno.shape[1], gram, every, out,
        (lower, start, first, second, partial, leaving, pairs[11]),
    )
    next(scores)
    next(here)
    next(scores)
    send.settle()
    next(here)
    next(scores)
    next(scores)
    next(cross)
    next(white)
    for _ in here:
        send.settle()
        next(cross)
    next(white)
    for _ in cross:
        send.settle()
    next(white)
    send.finish()


def shards(dosage, pheno, perm, snp_weight):
    snps, own = dosage.shape
    genes = pheno.shape[1]
    groups = lax.axis_size(SAMP)
    nulls = perm.shape[0]
    copies = nulls + 1
    rows = copies * snps
    cols = genes // groups
    samples = own * groups
    share = -(-rows // (16 * groups)) * 16
    tiles = 10
    most = max(n for _, n in CUTS) * 2 * TILE
    dma = pltpu.SemaphoreType.DMA
    vmem = pl.BlockSpec(memory_space=pltpu.VMEM)
    hbm = pl.BlockSpec(memory_space=pltpu.HBM)
    plain = [
        pltpu.VMEM((snps + 2 * nulls, samples), BF16),
        pltpu.VMEM((2 * nulls, samples), F32),
        pltpu.VMEM((LEAD + rows, samples), BF16),
        pltpu.VMEM((samples, cols), BF16),
        pltpu.VMEM((cols, rows - snps), BF16),
        pltpu.VMEM((rows - snps, 3 * cols), BF16),
        pltpu.VMEM((tiles * 2 * TILE, LANES), BF16),
        pltpu.VMEM((groups, share * groups, cols), BF16),
        pltpu.VMEM((2, 3, most // 4, LANES), BF16),
        pltpu.VMEM((2, most // 4, LANES), BF16),
        pltpu.VMEM((2, 16, most // 64, LANES), BF16),
        pltpu.VMEM((2, most // 64, LANES), BF16),
        pltpu.VMEM((groups, tiles * 2 * TILE, LANES), BF16),
        pltpu.VMEM((genes // TILE, TILE, 3 * TILE), BF16),
        *[pltpu.VMEM((genes, LANES), BF16)] * 3,
        pltpu.VMEM((genes, LANES), F32),
        pltpu.VMEM((3, share, cols), BF16),
        pltpu.VMEM(dosage.shape, jnp.int32),
        pltpu.VMEM(perm.shape, jnp.int32),
    ]
    each = len(CUTS)
    counts = [3, 5, 3, 3, 3, *[n * each for n in (3, 15, 15, 3, 8, 8)], 3]
    pairs = [dma((n,)) for n in counts for _ in range(2)]
    sizes = (len(plain), len(pairs), 1)
    white = pl.pallas_call(
        functools.partial(kernel, sizes, nulls * snps * lax.axis_size(SNP)),
        out_shape=jax.ShapeDtypeStruct((share * groups, cols), BF16),
        in_specs=[hbm, hbm, hbm, vmem],
        out_specs=vmem,
        scratch_shapes=[*plain, *pairs, dma((7,))],
        compiler_params=pltpu.CompilerParams(
            collective_id=0, has_side_effects=True, vmem_limit_bytes=60 << 20
        ),
        name="whitened_scores",
    )(dosage, pheno, perm, snp_weight[None, :])
    return white[:rows].reshape(copies, snps, cols)


def solution(mesh):
    finer = Mesh(mesh.devices.reshape(2, 2, 4, 8, 2), (*SAMP, *SNP))
    in_specs = (P(SNP, SAMP), P(SAMP, None), P(None, SAMP), P(SNP))
    return jax.shard_map(
        shards, mesh=finer, in_specs=in_specs, out_specs=P(None, SNP, SAMP), check_vma=False
    )
```

```python
import functools

import jax
import jax.numpy as jnp
from jax import lax
from jax.experimental import pallas as pl
from jax.experimental.pallas import tpu as pltpu
from jax.sharding import Mesh
from jax.sharding import PartitionSpec as P

SAMP = ("y_lo", "core")
SNP = ("x", "z", "y_hi")
F32 = jnp.float32
BF16 = jnp.bfloat16
NT = (((1,), (1,)), ((), ()))
LOW = 256
TILE = 256
LANES = 128
LEAD = 16
CHUNKS = 3
CUTS = ((0, 6), (6, 4))
MESH = pl.DeviceIdType.MESH


def span(index, size):
    return pl.ds(pl.multiple_of(index * size, size), size)


class Sender:
    def __init__(self):
        self.started, self.older = [], []

    def __call__(self, src, dst, sems, i, there):
        copy = pltpu.make_async_remote_copy(
            src_ref=src, dst_ref=dst, send_sem=sems[0].at[i], recv_sem=sems[1].at[i],
            device_id=there, device_id_type=MESH,
        )
        copy.start()
        self.started.append(copy)
        return copy

    def settle(self):
        for copy in self.older:
            copy.wait_send()
        self.started, self.older = [], self.started

    def finish(self):
        for copy in self.older + self.started:
            copy.wait_send()


class Place:
    def __init__(self):
        x, z, y_hi = lax.axis_index("x"), lax.axis_index("z"), lax.axis_index("y_hi")
        y_lo, core = lax.axis_index("y_lo"), lax.axis_index("core")
        self.x, self.z, self.y_hi, self.y_lo, self.core = x, z, y_hi, y_lo, core
        self.me = y_lo * 2 + core
        self.sib_id = y_lo * 2 + 1 - core
        self.near_id = (1 - y_lo) * 2 + core
        self.cross_id = (1 - y_lo) * 2 + 1 - core
        self.sibling = {"core": 1 - core}
        self.near = {"y_lo": 1 - y_lo}
        self.cross = {"y_lo": 1 - y_lo, "core": 1 - core}
        self.far = {"y_lo": 1 - y_lo, "y_hi": 1 - y_hi}
        self.far_cross = {"y_lo": 1 - y_lo, "y_hi": 1 - y_hi, "core": 1 - core}
        self.right, self.left = lax.rem(x + 1, 4), lax.rem(x + 3, 4)
        self.across = lax.rem(x + 2, 4)
        self.to_right, self.to_left = {"x": self.right}, {"x": self.left}
        peers = [(dz, dy) for dz in range(8) for dy in range(2) if dz or dy]
        self.peers = sorted(peers, key=lambda p: -min(p[0], 8 - p[0]) - 2 * p[1])

    def peer(self, dz, dy):
        there = {"z": lax.rem(self.z + dz, 8)}
        if dy:
            there["y_hi"] = 1 - self.y_hi
        return there


def score_steps(at, send, dosage, pheno, snp_weight, part, every, scratch):
    coded, codes, placed, cols_in, turned, near_w, a, p, s, n, f, own_sem = scratch
    snps, own = dosage.shape
    samples, cols = cols_in.shape
    nulls = codes.shape[0] // 2
    copies = nulls + 1
    mine = span(at.me, own)
    coming = [
        send(coded.at[:, mine], coded.at[:, mine], a, i, there)
        for i, there in enumerate((at.near, at.cross, at.sibling))
    ]
    cut = own * 7 // 16
    pheno_coming = []
    for i, (there, target, first, size) in enumerate(
        (
            (at.near, at.near_id, 0, cut), (at.far, at.near_id, cut, own - cut),
            (at.cross, at.cross_id, 0, cut), (at.far_cross, at.cross_id, cut, own - cut),
        )
    ):
        pheno_coming.append(
            send(
                pheno.at[pl.ds(first, size), span(target, cols)],
                cols_in.at[pl.ds(pl.multiple_of(at.me * own + first, 32), size)],
                p, i, there,
            )
        )
    pheno_coming.append(
        send(pheno.at[:, span(at.sib_id, cols)], cols_in.at[mine], p, 4, at.sibling)
    )
    stay = pltpu.make_async_copy(pheno.at[:, span(at.me, cols)], cols_in.at[mine], own_sem)
    stay.start()
    placed[:LEAD, :] = jnp.ones((LEAD, samples), BF16)
    for owner in range(4):
        every[owner, copies * snps :] = jnp.zeros((every.shape[1] - copies * snps, cols), BF16)
    for copy in coming:
        copy.wait_recv()

    codes[...] = coded[snps:, :].astype(F32)
    dose = coded[:snps, :]
    placed[LEAD : LEAD + snps, :] = dose
    dose32 = dose.astype(F32)
    dose_mean = jnp.sum(dose32, axis=1, keepdims=True) / samples
    dose_square = jnp.sum(dose32 * dose32, axis=1, keepdims=True) / samples
    spread_rows = jnp.sqrt(samples * (dose_square + 1e-05))
    steps = samples // LOW

    @pl.loop(0, nulls)
    def _(k):
        high = codes[pl.ds(k, 1), :]
        low = codes[pl.ds(nulls + k, 1), :]
        values = coded[:snps, :]
        masked = jnp.concatenate(
            [values * (high == F32(h)).astype(F32).astype(BF16) for h in range(steps)], axis=0
        )
        ids = lax.broadcasted_iota(jnp.int32, (LOW, samples), 0).astype(F32)
        onehot = (ids == low).astype(F32).astype(BF16)
        got = lax.dot_general(masked, onehot, NT, preferred_element_type=F32).astype(BF16)
        rows = pl.ds(pl.multiple_of(LEAD + (k + 1) * snps, 16), snps)
        for h in range(steps):
            placed[rows, h * LOW : (h + 1) * LOW] = got[h * snps : (h + 1) * snps]

    stay.wait()
    for copy in pheno_coming:
        copy.wait_recv()

    per = copies // CHUNKS
    total = None
    to_sib, to_near = [], []
    for c in range(CHUNKS):
        first = 0 if c == 0 else LEAD + c * per * snps
        last = LEAD + (c + 1) * per * snps
        raw = jnp.dot(placed[first:last, :], cols_in[...], preferred_element_type=F32)
        if c == 0:
            total = raw[:1]
            raw = raw[LEAD:]
        for j in range(per):
            value = (raw[j * snps : (j + 1) * snps] - dose_mean * total) / spread_rows
            row = (c * per + j) * snps
            every[at.me, row : row + snps] = value.astype(BF16)
        block = every.at[at.me, pl.ds(c * per * snps, per * snps)]
        to_near.append(send(block, block, n, c, at.near))
        to_sib.append(send(block, block, s, c, at.sibling))

    end = copies * snps
    turned[...] = every[at.me, snps:end].astype(F32).T.astype(BF16)
    spot = lax.broadcasted_iota(jnp.int32, (snps, snps), 0)
    spot = spot == lax.broadcasted_iota(jnp.int32, (snps, snps), 1)
    weight = jnp.sum(jnp.where(spot, snp_weight[...], F32(0)), axis=1, keepdims=True)

    def weigh(r, which):
        for k in range(nulls):
            value = every[which, (k + 1) * snps : (k + 2) * snps].astype(F32) * weight
            near_w[k * snps : (k + 1) * snps, r * cols : (r + 1) * cols] = value.astype(BF16)

    def tile(row, i, first):
        got = jnp.dot(
            turned[i * TILE : (i + 1) * TILE, :],
            near_w[:, pl.ds(pl.multiple_of(first, TILE), TILE)], preferred_element_type=F32,
        )
        got = got.astype(BF16)
        for h in range(2):
            at_row = (2 * row + h) * TILE
            part[at_row : at_row + TILE, :] = got[:, h * LANES : (h + 1) * LANES]

    weigh(0, at.me)
    for copy in to_sib:
        copy.wait_recv()
    weigh(1, at.sib_id)
    for i in range(2):
        for t in range(2):
            tile(i * 3 + t, i, t * TILE)
        tile(i * 3 + 2, i, cols + lax.rem(i + at.core, 2) * TILE)
    yield
    passed = []

    def hand_on(c):
        to_near[c].wait_recv()
        block = every.at[at.near_id, pl.ds(c * per * snps, per * snps)]
        passed.append(send(block, block, f, c, at.sibling))

    hand_on(0)
    hand_on(1)
    yield
    hand_on(2)
    yield
    for copy in passed:
        copy.wait_recv()
    weigh(2, (1 - at.y_lo) * 2 + lax.rem(at.core + at.y_lo, 2))
    for i in range(2):
        for t in range(2):
            tile(6 + i * 2 + t, i, 2 * cols + t * TILE)
    yield


def spread_chunk(at, send, total, part, gram, scratch, k):
    x_slots, acc, slots, chunk, xr, rr, gr, xg, ys, cs, own_in, own_out = scratch
    base, rows = (n * 2 * TILE for n in CUTS[k])
    block, half, bit = rows // 4, rows // 8, rows // 64
    x, z, y_hi = at.x, at.z, at.y_hi
    right, left, across = at.right, at.left, at.across
    x_slots, acc = x_slots.at[k], acc.at[k]
    slots, chunk = slots.at[k], chunk.at[k, pl.ds(0, bit)]

    def slot(i):
        return x_slots.at[i, pl.ds(0, block)]

    def x_sent(i, src, there):
        return send(src, slot(i), xr, 3 * k + i, there)

    def added(dst, sources):
        @pl.loop(0, block, step=64)
        def _(r):
            rows_at = pl.ds(pl.multiple_of(r, 64), 64)
            value = sources[0][rows_at, :].astype(F32)
            for source in sources[1:]:
                value += source[rows_at, :].astype(F32)
            dst[rows_at, :] = value.astype(BF16)

    def block_of(owner):
        return part.at[pl.ds(pl.multiple_of(base + owner * block, 128), block)]

    across_way = {"x": across}
    arrive = [
        x_sent(i, block_of(owner), there)
        for i, (owner, there) in enumerate(
            ((across, across_way), (right, at.to_right), (left, at.to_left))
        )
    ]
    yield
    for copy in arrive:
        copy.wait_recv()
    added(acc.at[pl.ds(0, block)], [block_of(x), slot(0), slot(1), slot(2)])

    def bit_at(at_y, at_z):
        return acc.at[pl.ds(pl.multiple_of((at_y * 8 + at_z) * bit, 16), bit)]

    arrive = []
    for i, (dz, dy) in enumerate(at.peers):
        at_y = 1 - y_hi if dy else y_hi
        src = bit_at(at_y, lax.rem(z + dz, 8))
        dst = slots.at[i, pl.ds(0, bit)]
        arrive.append(send(src, dst, rr, 15 * k + i, at.peer(dz, dy)))
    stay = pltpu.make_async_copy(bit_at(y_hi, z), slots.at[15, pl.ds(0, bit)], own_in.at[k])
    stay.start()
    yield
    stay.wait()
    value = slots[15, :bit].astype(F32)
    for i, copy in enumerate(arrive):
        copy.wait_recv()
        value += slots[i, :bit].astype(F32)
    chunk[...] = (value / total).astype(BF16)

    piece = at.me
    first = base + x * block + (y_hi * 8 + z) * bit
    dst = gram.at[piece, pl.ds(pl.multiple_of(first, 16), bit)]
    arrive = []
    for i, (dz, dy) in enumerate(at.peers):
        arrive.append(send(chunk, dst, gr, 15 * k + i, at.peer(dz, dy)))
    stay = pltpu.make_async_copy(chunk, dst, own_out.at[k])
    stay.start()
    yield
    stay.wait()
    for copy in arrive:
        copy.wait_recv()

    def at_half(which, owner, h):
        return gram.at[which, pl.ds(pl.multiple_of(base + owner * block + h * half, 64), half)]

    def at_block(which, owner):
        return gram.at[which, pl.ds(pl.multiple_of(base + owner * block, 128), block)]

    def to_x(i, src, there):
        return send(src, src, xg, 3 * k + i, there)

    c_all = []

    def to_sibling(which, owner):
        src = at_block(which, owner)
        c_all.append(send(src, src, cs, 8 * k + len(c_all), at.sibling))

    def to_y(i, owner, h):
        src = at_half(piece, owner, h)
        return send(src, src, ys, 8 * k + 2 * i + h, at.far if h else at.near)

    def from_y(copies, owner):
        for copy in copies:
            copy.wait_recv()
        to_sibling(at.near_id, owner)

    ways = ((at.to_right, left), (at.to_left, right), (across_way, across))
    x_coming = [to_x(i, at_block(piece, x), there) for i, (there, _) in enumerate(ways)]
    y_own = [to_y(0, x, h) for h in range(2)]
    to_sibling(piece, x)
    yield
    y_coming = []
    for i, (copy, (_, owner)) in enumerate(zip(x_coming, ways)):
        copy.wait_recv()
        y_coming.append([to_y(i + 1, owner, h) for h in range(2)])
        to_sibling(piece, owner)
    from_y(y_own, x)
    yield
    for copies, (_, owner) in zip(y_coming, ways):
        from_y(copies, owner)
    yield
    for copy in c_all:
        copy.wait_recv()


def white_steps(at, send, genes, gram, every, out, scratch):
    lower, start, first, second, partial, leaving, os = scratch
    cols = every.shape[2]
    share = leaving.shape[1]
    pieces = 4

    mine = span(at.me, share)
    for b in range(pieces):
        block = every[b, mine].astype(F32)
        block = jnp.concatenate([block, jnp.zeros((LANES - share, cols), F32)], axis=0)
        start[b * cols : (b + 1) * cols, :] = block.T.astype(BF16)
    yield

    def strip(a, row):
        first, last = 2 * row * TILE, 2 * (row + 1) * TILE
        halves = gram[a, first : first + TILE, :], gram[a, first + TILE : last, :]
        return jnp.concatenate(halves, axis=1)

    def flipped(a, row):
        return strip(a, row).astype(F32).T.astype(BF16)

    def product(tile, left, j):
        return jnp.dot(tile, left[span(j, TILE), :], preferred_element_type=F32)

    def places(a, i):
        c, y = lax.rem(a, 2), a // 2
        pair = 2 * (2 * y + 1 - c) + lax.rem(i + c, 2)
        rest = 2 * (2 * y + 1 - c) + 1 - lax.rem(i + c, 2)
        direct = 2 * (1 - y) + lax.rem(c + y, 2)
        turned = 2 * (1 - y) + 1 - lax.rem(c + y, 2)
        return pair, rest, direct, turned

    spot = lax.broadcasted_iota(jnp.int32, (TILE, TILE), 0)
    spot = spot == lax.broadcasted_iota(jnp.int32, (TILE, TILE), 1)
    trace = F32(0)
    for a in range(pieces):
        for i in range(2):
            trace += jnp.sum(jnp.where(spot, strip(a, i * 3 + i).astype(F32), F32(0)))
    scale = jnp.full((1, LANES), trace / genes + 1e-06, F32)
    inverse = 1.0 / scale
    rsqrt = 1.0 / jnp.sqrt(scale)

    @pl.loop(0, pieces)
    def _(a):
        for i in range(2):
            lower[places(a, i)[0], :, :TILE] = flipped(a, i * 3 + 2)

    def on_chip(left, a, i):
        pair, rest, _, _ = places(a, i)
        value = product(strip(a, i * 3), left, 2 * a)
        value += product(strip(a, i * 3 + 1), left, 2 * a + 1)
        value += product(strip(a, i * 3 + 2), left, pair)
        return value + product(lower[2 * a + i, :, :TILE], left, rest)

    def off_chip(left, a, i):
        _, _, direct, turned = places(a, i)
        value = None
        for t in range(2):
            one = product(strip(a, 6 + i * 2 + t), left, 2 * direct + t)
            one += product(lower[2 * a + i, :, (t + 1) * TILE : (t + 2) * TILE], left, 2 * turned + t)
            value = one if value is None else value + one
        return value

    def image(left, a, i):
        return (on_chip(left, a, i) + off_chip(left, a, i)) * inverse

    def own(source, a, i):
        return source[span(2 * a + i, TILE), :].astype(F32)

    @pl.loop(0, pieces)
    def _(a):
        for i in range(2):
            partial[span(2 * a + i, TILE), :] = on_chip(start, a, i)

    def absorb(a):
        for i in range(2):
            direct = places(a, i)[2]
            for t in range(2):
                row = 6 + i * 2 + t
                turned = flipped(a, row)
                lower[2 * direct + t, :, (i + 1) * TILE : (i + 2) * TILE] = turned
                partial[span(2 * a + i, TILE), :] += product(strip(a, row), start, 2 * direct + t)
                partial[span(2 * direct + t, TILE), :] += product(turned, start, 2 * a + i)

    yield
    absorb(at.me)
    yield
    absorb(at.near_id)
    yield
    absorb(at.sib_id)
    absorb(at.cross_id)

    @pl.loop(0, pieces)
    def _(a):
        for i in range(2):
            value = partial[span(2 * a + i, TILE), :] * inverse
            first[span(2 * a + i, TILE), :] = (1.5 * own(start, a, i) - 0.5 * value).astype(BF16)

    @pl.loop(0, pieces)
    def _(a):
        for i in range(2):
            second[span(2 * a + i, TILE), :] = image(first, a, i).astype(BF16)

    @pl.loop(0, pieces)
    def _(a):
        for i in range(2):
            inner = 1.5 * own(second, a, i) - 0.5 * image(second, a, i)
            first[span(2 * a + i, TILE), :] = (1.5 * own(start, a, i) - 0.5 * inner).astype(BF16)

    coming = []
    targets = ((at.near_id, at.near), (at.cross_id, at.cross), (at.sib_id, at.sibling))
    for t, (a, there) in enumerate((*targets, (at.me, None))):
        for i in range(2):
            value = (1.5 * own(first, a, i) - 0.5 * image(first, a, i)) * rsqrt
            value = value.T[:share].astype(BF16)
            cols_at = slice(i * TILE, (i + 1) * TILE)
            if there is None:
                out[mine, cols_at] = value
            else:
                leaving[t, :, cols_at] = value
        if there is not None:
            coming.append(send(leaving.at[t], out.at[mine], os, t, there))
    send.settle()
    for copy in coming:
        copy.wait_recv()
    yield


def kernel(sizes, total, dosage, pheno, perm, snp_weight, out, *scratch):
    refs, position = [], 0
    for size in sizes:
        refs.append(scratch[position : position + size])
        position += size
    plain, pairs, (singles,) = refs
    pairs = [(pairs[i], pairs[i + 1]) for i in range(0, len(pairs), 2)]
    (
        coded, codes, placed, cols_in, turned, near_w, part, every,
        x_slots, acc, slots, chunk, gram, lower, start, first, second, partial, leaving,
        dose_here, perm_here,
    ) = plain
    at, send = Place(), Sender()
    barrier = pltpu.get_barrier_semaphore()
    greeted = [at.sibling, at.near, at.cross, at.far, at.far_cross]
    greeted += [at.to_right, at.to_left, {"x": at.across}]
    greeted += [at.peer(*p) for p in at.peers]
    for there in greeted:
        pl.semaphore_signal(barrier, inc=1, device_id=there, device_id_type=MESH)
    snps, own = dosage.shape
    mine = span(at.me, own)
    loads = [
        pltpu.make_async_copy(dosage, dose_here, singles.at[1]),
        pltpu.make_async_copy(perm, perm_here, singles.at[2]),
    ]
    for load in loads:
        load.start()
    for load in loads:
        load.wait()
    coded[:snps, mine] = dose_here[...].astype(F32).astype(BF16)
    source = perm_here[...]
    both = jnp.concatenate([lax.shift_right_logical(source, 8), source & 255], axis=0)
    coded[snps:, mine] = both.astype(F32).astype(BF16)
    pl.semaphore_wait(barrier, len(greeted))
    scores = score_steps(
        at, send, dosage, pheno, snp_weight, part, every,
        (coded, codes, placed, cols_in, turned, near_w, *pairs[:5], singles.at[0]),
    )
    moved = (
        x_slots, acc, slots, chunk, *pairs[5:11], singles.at[pl.ds(3, 2)], singles.at[pl.ds(5, 2)],
    )
    here, cross = (spread_chunk(at, send, total, part, gram, moved, k) for k in range(2))
    white = white_steps(
        at, send, pheno.shape[1], gram, every, out,
        (lower, start, first, second, partial, leaving, pairs[11]),
    )
    next(scores)
    next(here)
    next(scores)
    send.settle()
    next(here)
    next(scores)
    next(scores)
    next(cross)
    next(white)
    for _ in here:
        send.settle()
        next(cross)
    next(white)
    next(white)
    for _ in cross:
        send.settle()
        next(white)
    next(white)
    send.finish()


def shards(dosage, pheno, perm, snp_weight):
    snps, own = dosage.shape
    genes = pheno.shape[1]
    groups = lax.axis_size(SAMP)
    nulls = perm.shape[0]
    copies = nulls + 1
    rows = copies * snps
    cols = genes // groups
    samples = own * groups
    share = -(-rows // (16 * groups)) * 16
    tiles = 10
    most = max(n for _, n in CUTS) * 2 * TILE
    dma = pltpu.SemaphoreType.DMA
    vmem = pl.BlockSpec(memory_space=pltpu.VMEM)
    hbm = pl.BlockSpec(memory_space=pltpu.HBM)
    plain = [
        pltpu.VMEM((snps + 2 * nulls, samples), BF16),
        pltpu.VMEM((2 * nulls, samples), F32),
        pltpu.VMEM((LEAD + rows, samples), BF16),
        pltpu.VMEM((samples, cols), BF16),
        pltpu.VMEM((cols, rows - snps), BF16),
        pltpu.VMEM((rows - snps, 3 * cols), BF16),
        pltpu.VMEM((tiles * 2 * TILE, LANES), BF16),
        pltpu.VMEM((groups, share * groups, cols), BF16),
        pltpu.VMEM((2, 3, most // 4, LANES), BF16),
        pltpu.VMEM((2, most // 4, LANES), BF16),
        pltpu.VMEM((2, 16, most // 64, LANES), BF16),
        pltpu.VMEM((2, most // 64, LANES), BF16),
        pltpu.VMEM((groups, tiles * 2 * TILE, LANES), BF16),
        pltpu.VMEM((genes // TILE, TILE, 3 * TILE), BF16),
        *[pltpu.VMEM((genes, LANES), BF16)] * 3,
        pltpu.VMEM((genes, LANES), F32),
        pltpu.VMEM((3, share, cols), BF16),
        pltpu.VMEM(dosage.shape, jnp.int32),
        pltpu.VMEM(perm.shape, jnp.int32),
    ]
    each = len(CUTS)
    counts = [3, 5, 3, 3, 3, *[n * each for n in (3, 15, 15, 3, 8, 8)], 3]
    pairs = [dma((n,)) for n in counts for _ in range(2)]
    sizes = (len(plain), len(pairs), 1)
    white = pl.pallas_call(
        functools.partial(kernel, sizes, nulls * snps * lax.axis_size(SNP)),
        out_shape=jax.ShapeDtypeStruct((share * groups, cols), BF16),
        in_specs=[hbm, hbm, hbm, vmem],
        out_specs=vmem,
        scratch_shapes=[*plain, *pairs, dma((7,))],
        compiler_params=pltpu.CompilerParams(
            collective_id=0, has_side_effects=True, vmem_limit_bytes=60 << 20
        ),
        name="whitened_scores",
    )(dosage, pheno, perm, snp_weight[None, :])
    return white[:rows].reshape(copies, snps, cols)


def solution(mesh):
    finer = Mesh(mesh.devices.reshape(2, 2, 4, 8, 2), (*SAMP, *SNP))
    in_specs = (P(SNP, SAMP), P(SAMP, None), P(None, SAMP), P(SNP))
    return jax.shard_map(
        shards, mesh=finer, in_specs=in_specs, out_specs=P(None, SNP, SAMP), check_vma=False
    )
```

```python
import functools

import jax
import jax.numpy as jnp
from jax import lax
from jax.experimental import pallas as pl
from jax.experimental.pallas import tpu as pltpu
from jax.sharding import Mesh
from jax.sharding import PartitionSpec as P

SAMP = ("y_lo", "core")
SNP = ("x", "z", "y_hi")
F32 = jnp.float32
BF16 = jnp.bfloat16
NT = (((1,), (1,)), ((), ()))
LOW = 256
TILE = 256
LANES = 128
LEAD = 16
CHUNKS = 3
CUTS = ((0, 6), (6, 4))
MESH = pl.DeviceIdType.MESH


def span(index, size):
    return pl.ds(pl.multiple_of(index * size, size), size)


class Sender:
    def __init__(self):
        self.started, self.older = [], []

    def __call__(self, src, dst, sems, i, there):
        copy = pltpu.make_async_remote_copy(
            src_ref=src, dst_ref=dst, send_sem=sems[0].at[i], recv_sem=sems[1].at[i],
            device_id=there, device_id_type=MESH,
        )
        copy.start()
        self.started.append(copy)
        return copy

    def settle(self):
        for copy in self.older:
            copy.wait_send()
        self.started, self.older = [], self.started

    def finish(self):
        for copy in self.older + self.started:
            copy.wait_send()


class Place:
    def __init__(self):
        x, z, y_hi = lax.axis_index("x"), lax.axis_index("z"), lax.axis_index("y_hi")
        y_lo, core = lax.axis_index("y_lo"), lax.axis_index("core")
        self.x, self.z, self.y_hi, self.y_lo, self.core = x, z, y_hi, y_lo, core
        self.me = y_lo * 2 + core
        self.sib_id = y_lo * 2 + 1 - core
        self.near_id = (1 - y_lo) * 2 + core
        self.cross_id = (1 - y_lo) * 2 + 1 - core
        self.sibling = {"core": 1 - core}
        self.near = {"y_lo": 1 - y_lo}
        self.cross = {"y_lo": 1 - y_lo, "core": 1 - core}
        self.far = {"y_lo": 1 - y_lo, "y_hi": 1 - y_hi}
        self.far_cross = {"y_lo": 1 - y_lo, "y_hi": 1 - y_hi, "core": 1 - core}
        self.right, self.left = lax.rem(x + 1, 4), lax.rem(x + 3, 4)
        self.across = lax.rem(x + 2, 4)
        self.to_right, self.to_left = {"x": self.right}, {"x": self.left}
        peers = [(dz, dy) for dz in range(8) for dy in range(2) if dz or dy]
        self.peers = sorted(peers, key=lambda p: -min(p[0], 8 - p[0]) - 2 * p[1])

    def peer(self, dz, dy):
        there = {"z": lax.rem(self.z + dz, 8)}
        if dy:
            there["y_hi"] = 1 - self.y_hi
        return there


def score_steps(at, send, dosage, pheno, snp_weight, part, every, scratch):
    coded, codes, placed, cols_in, turned, near_w, a, p, s, n, f, own_sem = scratch
    snps, own = dosage.shape
    samples, cols = cols_in.shape
    nulls = codes.shape[0] // 2
    copies = nulls + 1
    mine = span(at.me, own)
    coming = [
        send(coded.at[:, mine], coded.at[:, mine], a, i, there)
        for i, there in enumerate((at.near, at.cross, at.sibling))
    ]
    cut = own * 7 // 16
    pheno_coming = []
    for i, (there, target, first, size) in enumerate(
        (
            (at.near, at.near_id, 0, cut), (at.far, at.near_id, cut, own - cut),
            (at.cross, at.cross_id, 0, cut), (at.far_cross, at.cross_id, cut, own - cut),
        )
    ):
        pheno_coming.append(
            send(
                pheno.at[pl.ds(first, size), span(target, cols)],
                cols_in.at[pl.ds(pl.multiple_of(at.me * own + first, 32), size)],
                p, i, there,
            )
        )
    pheno_coming.append(
        send(pheno.at[:, span(at.sib_id, cols)], cols_in.at[mine], p, 4, at.sibling)
    )
    stay = pltpu.make_async_copy(pheno.at[:, span(at.me, cols)], cols_in.at[mine], own_sem)
    stay.start()
    placed[:LEAD, :] = jnp.ones((LEAD, samples), BF16)
    for owner in range(4):
        every[owner, copies * snps :] = jnp.zeros((every.shape[1] - copies * snps, cols), BF16)
    for copy in coming:
        copy.wait_recv()

    codes[...] = coded[snps:, :].astype(F32)
    dose = coded[:snps, :]
    placed[LEAD : LEAD + snps, :] = dose
    dose32 = dose.astype(F32)
    dose_mean = jnp.sum(dose32, axis=1, keepdims=True) / samples
    dose_square = jnp.sum(dose32 * dose32, axis=1, keepdims=True) / samples
    spread_rows = jnp.sqrt(samples * (dose_square + 1e-05))
    steps = samples // LOW

    @pl.loop(0, nulls)
    def _(k):
        high = codes[pl.ds(k, 1), :]
        low = codes[pl.ds(nulls + k, 1), :]
        values = coded[:snps, :]
        masked = jnp.concatenate(
            [values * (high == F32(h)).astype(F32).astype(BF16) for h in range(steps)], axis=0
        )
        ids = lax.broadcasted_iota(jnp.int32, (LOW, samples), 0).astype(F32)
        onehot = (ids == low).astype(F32).astype(BF16)
        got = lax.dot_general(masked, onehot, NT, preferred_element_type=F32).astype(BF16)
        rows = pl.ds(pl.multiple_of(LEAD + (k + 1) * snps, 16), snps)
        for h in range(steps):
            placed[rows, h * LOW : (h + 1) * LOW] = got[h * snps : (h + 1) * snps]

    stay.wait()
    for copy in pheno_coming:
        copy.wait_recv()

    per = copies // CHUNKS
    total = None
    to_sib, to_near = [], []
    for c in range(CHUNKS):
        first = 0 if c == 0 else LEAD + c * per * snps
        last = LEAD + (c + 1) * per * snps
        raw = jnp.dot(placed[first:last, :], cols_in[...], preferred_element_type=F32)
        if c == 0:
            total = raw[:1]
            raw = raw[LEAD:]
        for j in range(per):
            value = (raw[j * snps : (j + 1) * snps] - dose_mean * total) / spread_rows
            row = (c * per + j) * snps
            every[at.me, row : row + snps] = value.astype(BF16)
        block = every.at[at.me, pl.ds(c * per * snps, per * snps)]
        to_near.append(send(block, block, n, c, at.near))
        to_sib.append(send(block, block, s, c, at.sibling))

    end = copies * snps
    turned[...] = every[at.me, snps:end].astype(F32).T.astype(BF16)
    spot = lax.broadcasted_iota(jnp.int32, (snps, snps), 0)
    spot = spot == lax.broadcasted_iota(jnp.int32, (snps, snps), 1)
    weight = jnp.sum(jnp.where(spot, snp_weight[...], F32(0)), axis=1, keepdims=True)

    def weigh(r, which):
        for k in range(nulls):
            value = every[which, (k + 1) * snps : (k + 2) * snps].astype(F32) * weight
            near_w[k * snps : (k + 1) * snps, r * cols : (r + 1) * cols] = value.astype(BF16)

    def tile(row, i, first):
        got = jnp.dot(
            turned[i * TILE : (i + 1) * TILE, :],
            near_w[:, pl.ds(pl.multiple_of(first, TILE), TILE)], preferred_element_type=F32,
        )
        got = got.astype(BF16)
        for h in range(2):
            at_row = (2 * row + h) * TILE
            part[at_row : at_row + TILE, :] = got[:, h * LANES : (h + 1) * LANES]

    weigh(0, at.me)
    for copy in to_sib:
        copy.wait_recv()
    weigh(1, at.sib_id)
    for i in range(2):
        for t in range(2):
            tile(i * 3 + t, i, t * TILE)
        tile(i * 3 + 2, i, cols + lax.rem(i + at.core, 2) * TILE)
    yield
    passed = []

    def hand_on(c):
        to_near[c].wait_recv()
        block = every.at[at.near_id, pl.ds(c * per * snps, per * snps)]
        passed.append(send(block, block, f, c, at.sibling))

    hand_on(0)
    hand_on(1)
    yield
    hand_on(2)
    yield
    for copy in passed:
        copy.wait_recv()
    weigh(2, (1 - at.y_lo) * 2 + lax.rem(at.core + at.y_lo, 2))
    for i in range(2):
        for t in range(2):
            tile(6 + i * 2 + t, i, 2 * cols + t * TILE)
    yield


def spread_chunk(at, send, total, part, gram, scratch, k):
    x_slots, acc, slots, chunk, xr, rr, gr, xg, ys, cs, own_in, own_out = scratch
    base, rows = (n * 2 * TILE for n in CUTS[k])
    block, half, bit = rows // 4, rows // 8, rows // 64
    x, z, y_hi = at.x, at.z, at.y_hi
    right, left, across = at.right, at.left, at.across
    x_slots, acc = x_slots.at[k], acc.at[k]
    slots, chunk = slots.at[k], chunk.at[k, pl.ds(0, bit)]

    def slot(i):
        return x_slots.at[i, pl.ds(0, block)]

    def x_sent(i, src, there):
        return send(src, slot(i), xr, 3 * k + i, there)

    def added(dst, sources):
        @pl.loop(0, block, step=64)
        def _(r):
            rows_at = pl.ds(pl.multiple_of(r, 64), 64)
            value = sources[0][rows_at, :].astype(F32)
            for source in sources[1:]:
                value += source[rows_at, :].astype(F32)
            dst[rows_at, :] = value.astype(BF16)

    def block_of(owner):
        return part.at[pl.ds(pl.multiple_of(base + owner * block, 128), block)]

    across_way = {"x": across}
    arrive = [
        x_sent(i, block_of(owner), there)
        for i, (owner, there) in enumerate(
            ((across, across_way), (right, at.to_right), (left, at.to_left))
        )
    ]
    yield
    for copy in arrive:
        copy.wait_recv()
    added(acc.at[pl.ds(0, block)], [block_of(x), slot(0), slot(1), slot(2)])

    def bit_at(at_y, at_z):
        return acc.at[pl.ds(pl.multiple_of((at_y * 8 + at_z) * bit, 16), bit)]

    arrive = []
    for i, (dz, dy) in enumerate(at.peers):
        at_y = 1 - y_hi if dy else y_hi
        src = bit_at(at_y, lax.rem(z + dz, 8))
        dst = slots.at[i, pl.ds(0, bit)]
        arrive.append(send(src, dst, rr, 15 * k + i, at.peer(dz, dy)))
    stay = pltpu.make_async_copy(bit_at(y_hi, z), slots.at[15, pl.ds(0, bit)], own_in.at[k])
    stay.start()
    yield
    stay.wait()
    value = slots[15, :bit].astype(F32)
    for i, copy in enumerate(arrive):
        copy.wait_recv()
        value += slots[i, :bit].astype(F32)
    chunk[...] = (value / total).astype(BF16)

    piece = at.me
    first = base + x * block + (y_hi * 8 + z) * bit
    dst = gram.at[piece, pl.ds(pl.multiple_of(first, 16), bit)]
    arrive = []
    for i, (dz, dy) in enumerate(at.peers):
        arrive.append(send(chunk, dst, gr, 15 * k + i, at.peer(dz, dy)))
    stay = pltpu.make_async_copy(chunk, dst, own_out.at[k])
    stay.start()
    yield
    stay.wait()
    for copy in arrive:
        copy.wait_recv()

    def at_half(which, owner, h):
        return gram.at[which, pl.ds(pl.multiple_of(base + owner * block + h * half, 64), half)]

    def at_block(which, owner):
        return gram.at[which, pl.ds(pl.multiple_of(base + owner * block, 128), block)]

    def to_x(i, src, there):
        return send(src, src, xg, 3 * k + i, there)

    c_all = []

    def to_sibling(which, owner):
        src = at_block(which, owner)
        c_all.append(send(src, src, cs, 8 * k + len(c_all), at.sibling))

    def to_y(i, owner, h):
        src = at_half(piece, owner, h)
        return send(src, src, ys, 8 * k + 2 * i + h, at.far if h else at.near)

    def from_y(copies, owner):
        for copy in copies:
            copy.wait_recv()
        to_sibling(at.near_id, owner)

    ways = ((at.to_right, left), (at.to_left, right), (across_way, across))
    x_coming = [to_x(i, at_block(piece, x), there) for i, (there, _) in enumerate(ways)]
    y_own = [to_y(0, x, h) for h in range(2)]
    to_sibling(piece, x)
    yield
    y_coming = []
    for i, (copy, (_, owner)) in enumerate(zip(x_coming, ways)):
        copy.wait_recv()
        y_coming.append([to_y(i + 1, owner, h) for h in range(2)])
    for _, owner in ways:
        to_sibling(piece, owner)
    from_y(y_own, x)
    yield
    for copies, (_, owner) in zip(y_coming, ways):
        from_y(copies, owner)
    yield
    for copy in c_all:
        copy.wait_recv()


def white_steps(at, send, genes, gram, every, out, scratch):
    lower, start, first, second, partial, leaving, os = scratch
    cols = every.shape[2]
    share = leaving.shape[1]
    pieces = 4

    mine = span(at.me, share)
    for b in range(pieces):
        block = every[b, mine].astype(F32)
        block = jnp.concatenate([block, jnp.zeros((LANES - share, cols), F32)], axis=0)
        start[b * cols : (b + 1) * cols, :] = block.T.astype(BF16)
    yield

    def strip(a, row):
        first, last = 2 * row * TILE, 2 * (row + 1) * TILE
        halves = gram[a, first : first + TILE, :], gram[a, first + TILE : last, :]
        return jnp.concatenate(halves, axis=1)

    def flipped(a, row):
        return strip(a, row).astype(F32).T.astype(BF16)

    def product(tile, left, j):
        return jnp.dot(tile, left[span(j, TILE), :], preferred_element_type=F32)

    def places(a, i):
        c, y = lax.rem(a, 2), a // 2
        pair = 2 * (2 * y + 1 - c) + lax.rem(i + c, 2)
        rest = 2 * (2 * y + 1 - c) + 1 - lax.rem(i + c, 2)
        direct = 2 * (1 - y) + lax.rem(c + y, 2)
        turned = 2 * (1 - y) + 1 - lax.rem(c + y, 2)
        return pair, rest, direct, turned

    spot = lax.broadcasted_iota(jnp.int32, (TILE, TILE), 0)
    spot = spot == lax.broadcasted_iota(jnp.int32, (TILE, TILE), 1)
    trace = F32(0)
    for a in range(pieces):
        for i in range(2):
            trace += jnp.sum(jnp.where(spot, strip(a, i * 3 + i).astype(F32), F32(0)))
    scale = jnp.full((1, LANES), trace / genes + 1e-06, F32)
    inverse = 1.0 / scale
    rsqrt = 1.0 / jnp.sqrt(scale)

    @pl.loop(0, pieces)
    def _(a):
        for i in range(2):
            lower[places(a, i)[0], :, :TILE] = flipped(a, i * 3 + 2)

    def on_chip(left, a, i):
        pair, rest, _, _ = places(a, i)
        value = product(strip(a, i * 3), left, 2 * a)
        value += product(strip(a, i * 3 + 1), left, 2 * a + 1)
        value += product(strip(a, i * 3 + 2), left, pair)
        return value + product(lower[2 * a + i, :, :TILE], left, rest)

    def off_chip(left, a, i):
        _, _, direct, turned = places(a, i)
        value = None
        for t in range(2):
            one = product(strip(a, 6 + i * 2 + t), left, 2 * direct + t)
            one += product(lower[2 * a + i, :, (t + 1) * TILE : (t + 2) * TILE], left, 2 * turned + t)
            value = one if value is None else value + one
        return value

    def image(left, a, i):
        return (on_chip(left, a, i) + off_chip(left, a, i)) * inverse

    def own(source, a, i):
        return source[span(2 * a + i, TILE), :].astype(F32)

    @pl.loop(0, pieces)
    def _(a):
        for i in range(2):
            partial[span(2 * a + i, TILE), :] = on_chip(start, a, i)

    def absorb(a):
        for i in range(2):
            direct = places(a, i)[2]
            for t in range(2):
                row = 6 + i * 2 + t
                turned = flipped(a, row)
                lower[2 * direct + t, :, (i + 1) * TILE : (i + 2) * TILE] = turned
                partial[span(2 * a + i, TILE), :] += product(strip(a, row), start, 2 * direct + t)
                partial[span(2 * direct + t, TILE), :] += product(turned, start, 2 * a + i)

    yield
    absorb(at.me)
    yield
    absorb(at.near_id)
    yield
    absorb(at.sib_id)
    absorb(at.cross_id)

    @pl.loop(0, pieces)
    def _(a):
        for i in range(2):
            value = partial[span(2 * a + i, TILE), :] * inverse
            first[span(2 * a + i, TILE), :] = (1.5 * own(start, a, i) - 0.5 * value).astype(BF16)

    @pl.loop(0, pieces)
    def _(a):
        for i in range(2):
            second[span(2 * a + i, TILE), :] = image(first, a, i).astype(BF16)

    @pl.loop(0, pieces)
    def _(a):
        for i in range(2):
            inner = 1.5 * own(second, a, i) - 0.5 * image(second, a, i)
            first[span(2 * a + i, TILE), :] = (1.5 * own(start, a, i) - 0.5 * inner).astype(BF16)

    coming = []
    targets = ((at.near_id, at.near), (at.cross_id, at.cross), (at.sib_id, at.sibling))
    for t, (a, there) in enumerate((*targets, (at.me, None))):
        for i in range(2):
            value = (1.5 * own(first, a, i) - 0.5 * image(first, a, i)) * rsqrt
            value = value.T[:share].astype(BF16)
            cols_at = slice(i * TILE, (i + 1) * TILE)
            if there is None:
                out[mine, cols_at] = value
                continue
            leaving[t, :, cols_at] = value
            dst = out.at[mine, cols_at]
            coming.append(send(leaving.at[t, :, cols_at], dst, os, 2 * t + i, there))
    send.settle()
    for copy in coming:
        copy.wait_recv()
    yield


def kernel(sizes, total, dosage, pheno, perm, snp_weight, out, *scratch):
    refs, position = [], 0
    for size in sizes:
        refs.append(scratch[position : position + size])
        position += size
    plain, pairs, (singles,) = refs
    pairs = [(pairs[i], pairs[i + 1]) for i in range(0, len(pairs), 2)]
    (
        coded, codes, placed, cols_in, turned, near_w, part, every,
        x_slots, acc, slots, chunk, gram, lower, start, first, second, partial, leaving,
        dose_here, perm_here,
    ) = plain
    at, send = Place(), Sender()
    barrier = pltpu.get_barrier_semaphore()
    greeted = [at.peer(*p) for p in at.peers]
    greeted += [{"x": at.across}, at.to_right, at.to_left]
    greeted += [at.far_cross, at.far, at.cross, at.near, at.sibling]
    for there in greeted:
        pl.semaphore_signal(barrier, inc=1, device_id=there, device_id_type=MESH)
    snps, own = dosage.shape
    mine = span(at.me, own)
    loads = [
        pltpu.make_async_copy(dosage, dose_here, singles.at[1]),
        pltpu.make_async_copy(perm, perm_here, singles.at[2]),
    ]
    for load in loads:
        load.start()
    for load in loads:
        load.wait()
    coded[:snps, mine] = dose_here[...].astype(F32).astype(BF16)
    source = perm_here[...]
    both = jnp.concatenate([lax.shift_right_logical(source, 8), source & 255], axis=0)
    coded[snps:, mine] = both.astype(F32).astype(BF16)
    pl.semaphore_wait(barrier, len(greeted))
    scores = score_steps(
        at, send, dosage, pheno, snp_weight, part, every,
        (coded, codes, placed, cols_in, turned, near_w, *pairs[:5], singles.at[0]),
    )
    moved = (
        x_slots, acc, slots, chunk, *pairs[5:11], singles.at[pl.ds(3, 2)], singles.at[pl.ds(5, 2)],
    )
    here, cross = (spread_chunk(at, send, total, part, gram, moved, k) for k in range(2))
    white = white_steps(
        at, send, pheno.shape[1], gram, every, out,
        (lower, start, first, second, partial, leaving, pairs[11]),
    )
    next(scores)
    next(here)
    next(scores)
    send.settle()
    next(here)
    next(scores)
    next(scores)
    next(cross)
    next(white)
    for _ in here:
        send.settle()
        next(cross)
    next(white)
    next(white)
    for _ in cross:
        send.settle()
        next(white)
    next(white)
    send.finish()


def shards(dosage, pheno, perm, snp_weight):
    snps, own = dosage.shape
    genes = pheno.shape[1]
    groups = lax.axis_size(SAMP)
    nulls = perm.shape[0]
    copies = nulls + 1
    rows = copies * snps
    cols = genes // groups
    samples = own * groups
    share = -(-rows // (16 * groups)) * 16
    tiles = 10
    most = max(n for _, n in CUTS) * 2 * TILE
    dma = pltpu.SemaphoreType.DMA
    vmem = pl.BlockSpec(memory_space=pltpu.VMEM)
    hbm = pl.BlockSpec(memory_space=pltpu.HBM)
    plain = [
        pltpu.VMEM((snps + 2 * nulls, samples), BF16),
        pltpu.VMEM((2 * nulls, samples), F32),
        pltpu.VMEM((LEAD + rows, samples), BF16),
        pltpu.VMEM((samples, cols), BF16),
        pltpu.VMEM((cols, rows - snps), BF16),
        pltpu.VMEM((rows - snps, 3 * cols), BF16),
        pltpu.VMEM((tiles * 2 * TILE, LANES), BF16),
        pltpu.VMEM((groups, share * groups, cols), BF16),
        pltpu.VMEM((2, 3, most // 4, LANES), BF16),
        pltpu.VMEM((2, most // 4, LANES), BF16),
        pltpu.VMEM((2, 16, most // 64, LANES), BF16),
        pltpu.VMEM((2, most // 64, LANES), BF16),
        pltpu.VMEM((groups, tiles * 2 * TILE, LANES), BF16),
        pltpu.VMEM((genes // TILE, TILE, 3 * TILE), BF16),
        *[pltpu.VMEM((genes, LANES), BF16)] * 3,
        pltpu.VMEM((genes, LANES), F32),
        pltpu.VMEM((3, share, cols), BF16),
        pltpu.VMEM(dosage.shape, jnp.int32),
        pltpu.VMEM(perm.shape, jnp.int32),
    ]
    each = len(CUTS)
    counts = [3, 5, 3, 3, 3, *[n * each for n in (3, 15, 15, 3, 8, 8)], 6]
    pairs = [dma((n,)) for n in counts for _ in range(2)]
    sizes = (len(plain), len(pairs), 1)
    white = pl.pallas_call(
        functools.partial(kernel, sizes, nulls * snps * lax.axis_size(SNP)),
        out_shape=jax.ShapeDtypeStruct((share * groups, cols), BF16),
        in_specs=[hbm, hbm, hbm, vmem],
        out_specs=vmem,
        scratch_shapes=[*plain, *pairs, dma((7,))],
        compiler_params=pltpu.CompilerParams(
            collective_id=0, has_side_effects=True, vmem_limit_bytes=60 << 20
        ),
        name="whitened_scores",
    )(dosage, pheno, perm, snp_weight[None, :])
    return white[:rows].reshape(copies, snps, cols)


def solution(mesh):
    finer = Mesh(mesh.devices.reshape(2, 2, 4, 8, 2), (*SAMP, *SNP))
    in_specs = (P(SNP, SAMP), P(SAMP, None), P(None, SAMP), P(SNP))
    return jax.shard_map(
        shards, mesh=finer, in_specs=in_specs, out_specs=P(None, SNP, SAMP), check_vma=False
    )
```

```python
import functools

import jax
import jax.numpy as jnp
from jax import lax
from jax.experimental import pallas as pl
from jax.experimental.pallas import tpu as pltpu
from jax.sharding import Mesh
from jax.sharding import PartitionSpec as P

SAMP = ("y_lo", "core")
SNP = ("x", "z", "y_hi")
F32 = jnp.float32
BF16 = jnp.bfloat16
NT = (((1,), (1,)), ((), ()))
LOW = 256
TILE = 256
LANES = 128
LEAD = 16
CHUNKS = 3
CUTS = ((0, 6), (6, 4))
MESH = pl.DeviceIdType.MESH


def span(index, size):
    return pl.ds(pl.multiple_of(index * size, size), size)


class Sender:
    def __init__(self):
        self.started, self.older = [], []

    def __call__(self, src, dst, sems, i, there):
        copy = pltpu.make_async_remote_copy(
            src_ref=src, dst_ref=dst, send_sem=sems[0].at[i], recv_sem=sems[1].at[i],
            device_id=there, device_id_type=MESH,
        )
        copy.start()
        self.started.append(copy)
        return copy

    def settle(self):
        for copy in self.older:
            copy.wait_send()
        self.started, self.older = [], self.started

    def finish(self):
        for copy in self.older + self.started:
            copy.wait_send()


class Place:
    def __init__(self):
        x, z, y_hi = lax.axis_index("x"), lax.axis_index("z"), lax.axis_index("y_hi")
        y_lo, core = lax.axis_index("y_lo"), lax.axis_index("core")
        self.x, self.z, self.y_hi, self.y_lo, self.core = x, z, y_hi, y_lo, core
        self.me = y_lo * 2 + core
        self.sib_id = y_lo * 2 + 1 - core
        self.near_id = (1 - y_lo) * 2 + core
        self.cross_id = (1 - y_lo) * 2 + 1 - core
        self.sibling = {"core": 1 - core}
        self.near = {"y_lo": 1 - y_lo}
        self.cross = {"y_lo": 1 - y_lo, "core": 1 - core}
        self.far = {"y_lo": 1 - y_lo, "y_hi": 1 - y_hi}
        self.far_cross = {"y_lo": 1 - y_lo, "y_hi": 1 - y_hi, "core": 1 - core}
        self.right, self.left = lax.rem(x + 1, 4), lax.rem(x + 3, 4)
        self.across = lax.rem(x + 2, 4)
        self.to_right, self.to_left = {"x": self.right}, {"x": self.left}
        peers = [(dz, dy) for dz in range(8) for dy in range(2) if dz or dy]
        self.peers = sorted(peers, key=lambda p: -min(p[0], 8 - p[0]) - 2 * p[1])

    def peer(self, dz, dy):
        there = {"z": lax.rem(self.z + dz, 8)}
        if dy:
            there["y_hi"] = 1 - self.y_hi
        return there


def score_steps(at, send, dosage, pheno, snp_weight, part, every, scratch):
    coded, codes, placed, cols_in, early, turned, near_w, a, p, s, n, f, own_sem = scratch
    snps, own = dosage.shape
    samples, cols = cols_in.shape
    nulls = codes.shape[0] // 2
    copies = nulls + 1
    mine = span(at.me, own)
    coming = [
        send(coded.at[:, mine], coded.at[:, mine], a, i, there)
        for i, there in enumerate((at.near, at.cross, at.sibling))
    ]
    cut = own * 7 // 16
    pheno_coming = []
    for i, (there, target, first, size) in enumerate(
        (
            (at.near, at.near_id, 0, cut), (at.far, at.near_id, cut, own - cut),
            (at.cross, at.cross_id, 0, cut), (at.far_cross, at.cross_id, cut, own - cut),
        )
    ):
        pheno_coming.append(
            send(
                pheno.at[pl.ds(first, size), span(target, cols)],
                cols_in.at[pl.ds(pl.multiple_of(at.me * own + first, 32), size)],
                p, i, there,
            )
        )
    pheno_coming.append(
        send(pheno.at[:, span(at.sib_id, cols)], cols_in.at[mine], p, 4, at.sibling)
    )
    stay = pltpu.make_async_copy(pheno.at[:, span(at.me, cols)], cols_in.at[mine], own_sem)
    stay.start()
    placed[:LEAD, :] = jnp.ones((LEAD, samples), BF16)
    for owner in range(4):
        every[owner, copies * snps :] = jnp.zeros((every.shape[1] - copies * snps, cols), BF16)
    for copy in coming:
        copy.wait_recv()

    codes[...] = coded[snps:, :].astype(F32)
    dose = coded[:snps, :]
    placed[LEAD : LEAD + snps, :] = dose
    dose32 = dose.astype(F32)
    dose_mean = jnp.sum(dose32, axis=1, keepdims=True) / samples
    dose_square = jnp.sum(dose32 * dose32, axis=1, keepdims=True) / samples
    spread_rows = jnp.sqrt(samples * (dose_square + 1e-05))
    steps = samples // LOW

    @pl.loop(0, nulls)
    def _(k):
        high = codes[pl.ds(k, 1), :]
        low = codes[pl.ds(nulls + k, 1), :]
        values = coded[:snps, :]
        masked = jnp.concatenate(
            [values * (high == F32(h)).astype(F32).astype(BF16) for h in range(steps)], axis=0
        )
        ids = lax.broadcasted_iota(jnp.int32, (LOW, samples), 0).astype(F32)
        onehot = (ids == low).astype(F32).astype(BF16)
        got = lax.dot_general(masked, onehot, NT, preferred_element_type=F32).astype(BF16)
        rows = pl.ds(pl.multiple_of(LEAD + (k + 1) * snps, 16), snps)
        for h in range(steps):
            placed[rows, h * LOW : (h + 1) * LOW] = got[h * snps : (h + 1) * snps]

    half = samples // 2
    here, there = span(at.y_lo, half), span(1 - at.y_lo, half)
    stay.wait()
    pheno_coming.pop().wait_recv()
    early[...] = jnp.dot(placed[:, here], cols_in[here, :], preferred_element_type=F32)
    for copy in pheno_coming:
        copy.wait_recv()

    per = copies // CHUNKS
    total = None
    to_sib, to_near = [], []
    for c in range(CHUNKS):
        first = 0 if c == 0 else LEAD + c * per * snps
        last = LEAD + (c + 1) * per * snps
        raw = early[first:last, :]
        raw += jnp.dot(placed[first:last, there], cols_in[there, :], preferred_element_type=F32)
        if c == 0:
            total = raw[:1]
            raw = raw[LEAD:]
        for j in range(per):
            value = (raw[j * snps : (j + 1) * snps] - dose_mean * total) / spread_rows
            row = (c * per + j) * snps
            every[at.me, row : row + snps] = value.astype(BF16)
        block = every.at[at.me, pl.ds(c * per * snps, per * snps)]
        to_near.append(send(block, block, n, c, at.near))
        to_sib.append(send(block, block, s, c, at.sibling))

    end = copies * snps
    turned[...] = every[at.me, snps:end].astype(F32).T.astype(BF16)
    spot = lax.broadcasted_iota(jnp.int32, (snps, snps), 0)
    spot = spot == lax.broadcasted_iota(jnp.int32, (snps, snps), 1)
    weight = jnp.sum(jnp.where(spot, snp_weight[...], F32(0)), axis=1, keepdims=True)

    def weigh(r, which):
        for k in range(nulls):
            value = every[which, (k + 1) * snps : (k + 2) * snps].astype(F32) * weight
            near_w[k * snps : (k + 1) * snps, r * cols : (r + 1) * cols] = value.astype(BF16)

    def tile(row, i, first):
        got = jnp.dot(
            turned[i * TILE : (i + 1) * TILE, :],
            near_w[:, pl.ds(pl.multiple_of(first, TILE), TILE)], preferred_element_type=F32,
        )
        got = got.astype(BF16)
        for h in range(2):
            at_row = (2 * row + h) * TILE
            part[at_row : at_row + TILE, :] = got[:, h * LANES : (h + 1) * LANES]

    weigh(0, at.me)
    for copy in to_sib:
        copy.wait_recv()
    weigh(1, at.sib_id)
    for i in range(2):
        for t in range(2):
            tile(i * 3 + t, i, t * TILE)
        tile(i * 3 + 2, i, cols + lax.rem(i + at.core, 2) * TILE)
    yield
    passed = []

    def hand_on(c):
        to_near[c].wait_recv()
        block = every.at[at.near_id, pl.ds(c * per * snps, per * snps)]
        passed.append(send(block, block, f, c, at.sibling))

    hand_on(0)
    hand_on(1)
    yield
    hand_on(2)
    yield
    for copy in passed:
        copy.wait_recv()
    weigh(2, (1 - at.y_lo) * 2 + lax.rem(at.core + at.y_lo, 2))
    for i in range(2):
        for t in range(2):
            tile(6 + i * 2 + t, i, 2 * cols + t * TILE)
    yield


def spread_chunk(at, send, total, part, gram, scratch, k):
    x_slots, acc, slots, chunk, xr, rr, gr, xg, ys, cs, own_in, own_out = scratch
    base, rows = (n * 2 * TILE for n in CUTS[k])
    block, half, bit = rows // 4, rows // 8, rows // 64
    x, z, y_hi = at.x, at.z, at.y_hi
    right, left, across = at.right, at.left, at.across
    x_slots, acc = x_slots.at[k], acc.at[k]
    slots, chunk = slots.at[k], chunk.at[k, pl.ds(0, bit)]

    def slot(i):
        return x_slots.at[i, pl.ds(0, block)]

    def x_sent(i, src, there):
        return send(src, slot(i), xr, 3 * k + i, there)

    def added(dst, sources):
        @pl.loop(0, block, step=64)
        def _(r):
            rows_at = pl.ds(pl.multiple_of(r, 64), 64)
            value = sources[0][rows_at, :].astype(F32)
            for source in sources[1:]:
                value += source[rows_at, :].astype(F32)
            dst[rows_at, :] = value.astype(BF16)

    def block_of(owner):
        return part.at[pl.ds(pl.multiple_of(base + owner * block, 128), block)]

    across_way = {"x": across}
    arrive = [
        x_sent(i, block_of(owner), there)
        for i, (owner, there) in enumerate(
            ((across, across_way), (right, at.to_right), (left, at.to_left))
        )
    ]
    yield
    for copy in arrive:
        copy.wait_recv()
    added(acc.at[pl.ds(0, block)], [block_of(x), slot(0), slot(1), slot(2)])

    def bit_at(at_y, at_z):
        return acc.at[pl.ds(pl.multiple_of((at_y * 8 + at_z) * bit, 16), bit)]

    arrive = []
    for i, (dz, dy) in enumerate(at.peers):
        at_y = 1 - y_hi if dy else y_hi
        src = bit_at(at_y, lax.rem(z + dz, 8))
        dst = slots.at[i, pl.ds(0, bit)]
        arrive.append(send(src, dst, rr, 15 * k + i, at.peer(dz, dy)))
    stay = pltpu.make_async_copy(bit_at(y_hi, z), slots.at[15, pl.ds(0, bit)], own_in.at[k])
    stay.start()
    yield
    stay.wait()
    value = slots[15, :bit].astype(F32)
    for i, copy in enumerate(arrive):
        copy.wait_recv()
        value += slots[i, :bit].astype(F32)
    chunk[...] = (value / total).astype(BF16)

    piece = at.me
    first = base + x * block + (y_hi * 8 + z) * bit
    dst = gram.at[piece, pl.ds(pl.multiple_of(first, 16), bit)]
    arrive = []
    for i, (dz, dy) in enumerate(at.peers):
        arrive.append(send(chunk, dst, gr, 15 * k + i, at.peer(dz, dy)))
    stay = pltpu.make_async_copy(chunk, dst, own_out.at[k])
    stay.start()
    yield
    stay.wait()
    for copy in arrive:
        copy.wait_recv()

    def at_half(which, owner, h):
        return gram.at[which, pl.ds(pl.multiple_of(base + owner * block + h * half, 64), half)]

    def at_block(which, owner):
        return gram.at[which, pl.ds(pl.multiple_of(base + owner * block, 128), block)]

    def to_x(i, src, there):
        return send(src, src, xg, 3 * k + i, there)

    c_all = []

    def to_sibling(which, owner):
        src = at_block(which, owner)
        c_all.append(send(src, src, cs, 8 * k + len(c_all), at.sibling))

    def to_y(i, owner, h):
        src = at_half(piece, owner, h)
        return send(src, src, ys, 8 * k + 2 * i + h, at.far if h else at.near)

    def from_y(copies, owner):
        for copy in copies:
            copy.wait_recv()
        to_sibling(at.near_id, owner)

    ways = ((at.to_right, left), (at.to_left, right), (across_way, across))
    x_coming = [to_x(i, at_block(piece, x), there) for i, (there, _) in enumerate(ways)]
    y_own = [to_y(0, x, h) for h in range(2)]
    to_sibling(piece, x)
    yield
    y_coming = []
    for i, (copy, (_, owner)) in enumerate(zip(x_coming, ways)):
        copy.wait_recv()
        y_coming.append([to_y(i + 1, owner, h) for h in range(2)])
    for _, owner in ways:
        to_sibling(piece, owner)
    from_y(y_own, x)
    yield
    for copies, (_, owner) in zip(y_coming, ways):
        from_y(copies, owner)
    yield
    for copy in c_all:
        copy.wait_recv()


def white_steps(at, send, genes, gram, every, out, scratch):
    lower, start, first, second, partial, leaving, os = scratch
    cols = every.shape[2]
    share = leaving.shape[1]
    pieces = 4

    mine = span(at.me, share)
    for b in range(pieces):
        block = every[b, mine].astype(F32)
        block = jnp.concatenate([block, jnp.zeros((LANES - share, cols), F32)], axis=0)
        start[b * cols : (b + 1) * cols, :] = block.T.astype(BF16)
    yield

    def strip(a, row):
        first, last = 2 * row * TILE, 2 * (row + 1) * TILE
        halves = gram[a, first : first + TILE, :], gram[a, first + TILE : last, :]
        return jnp.concatenate(halves, axis=1)

    def flipped(a, row):
        return strip(a, row).astype(F32).T.astype(BF16)

    def product(tile, left, j):
        return jnp.dot(tile, left[span(j, TILE), :], preferred_element_type=F32)

    def places(a, i):
        c, y = lax.rem(a, 2), a // 2
        pair = 2 * (2 * y + 1 - c) + lax.rem(i + c, 2)
        rest = 2 * (2 * y + 1 - c) + 1 - lax.rem(i + c, 2)
        direct = 2 * (1 - y) + lax.rem(c + y, 2)
        turned = 2 * (1 - y) + 1 - lax.rem(c + y, 2)
        return pair, rest, direct, turned

    spot = lax.broadcasted_iota(jnp.int32, (TILE, TILE), 0)
    spot = spot == lax.broadcasted_iota(jnp.int32, (TILE, TILE), 1)
    trace = F32(0)
    for a in range(pieces):
        for i in range(2):
            trace += jnp.sum(jnp.where(spot, strip(a, i * 3 + i).astype(F32), F32(0)))
    scale = jnp.full((1, LANES), trace / genes + 1e-06, F32)
    inverse = 1.0 / scale
    rsqrt = 1.0 / jnp.sqrt(scale)

    @pl.loop(0, pieces)
    def _(a):
        for i in range(2):
            lower[places(a, i)[0], :, :TILE] = flipped(a, i * 3 + 2)

    def on_chip(left, a, i):
        pair, rest, _, _ = places(a, i)
        value = product(strip(a, i * 3), left, 2 * a)
        value += product(strip(a, i * 3 + 1), left, 2 * a + 1)
        value += product(strip(a, i * 3 + 2), left, pair)
        return value + product(lower[2 * a + i, :, :TILE], left, rest)

    def off_chip(left, a, i):
        _, _, direct, turned = places(a, i)
        value = None
        for t in range(2):
            one = product(strip(a, 6 + i * 2 + t), left, 2 * direct + t)
            one += product(lower[2 * a + i, :, (t + 1) * TILE : (t + 2) * TILE], left, 2 * turned + t)
            value = one if value is None else value + one
        return value

    def image(left, a, i):
        return (on_chip(left, a, i) + off_chip(left, a, i)) * inverse

    def own(source, a, i):
        return source[span(2 * a + i, TILE), :].astype(F32)

    @pl.loop(0, pieces)
    def _(a):
        for i in range(2):
            partial[span(2 * a + i, TILE), :] = on_chip(start, a, i)

    def absorb(a):
        for i in range(2):
            direct = places(a, i)[2]
            for t in range(2):
                row = 6 + i * 2 + t
                turned = flipped(a, row)
                lower[2 * direct + t, :, (i + 1) * TILE : (i + 2) * TILE] = turned
                partial[span(2 * a + i, TILE), :] += product(strip(a, row), start, 2 * direct + t)
                partial[span(2 * direct + t, TILE), :] += product(turned, start, 2 * a + i)

    yield
    absorb(at.me)
    yield
    absorb(at.near_id)
    yield
    absorb(at.sib_id)
    absorb(at.cross_id)

    @pl.loop(0, pieces)
    def _(a):
        for i in range(2):
            value = partial[span(2 * a + i, TILE), :] * inverse
            first[span(2 * a + i, TILE), :] = (1.5 * own(start, a, i) - 0.5 * value).astype(BF16)

    @pl.loop(0, pieces)
    def _(a):
        for i in range(2):
            second[span(2 * a + i, TILE), :] = image(first, a, i).astype(BF16)

    @pl.loop(0, pieces)
    def _(a):
        for i in range(2):
            inner = 1.5 * own(second, a, i) - 0.5 * image(second, a, i)
            first[span(2 * a + i, TILE), :] = (1.5 * own(start, a, i) - 0.5 * inner).astype(BF16)

    coming = []
    targets = ((at.near_id, at.near), (at.cross_id, at.cross), (at.sib_id, at.sibling))
    for t, (a, there) in enumerate((*targets, (at.me, None))):
        for i in range(2):
            value = (1.5 * own(first, a, i) - 0.5 * image(first, a, i)) * rsqrt
            value = value.T[:share].astype(BF16)
            cols_at = slice(i * TILE, (i + 1) * TILE)
            if there is None:
                out[mine, cols_at] = value
                continue
            leaving[t, :, cols_at] = value
            dst = out.at[mine, cols_at]
            coming.append(send(leaving.at[t, :, cols_at], dst, os, 2 * t + i, there))
    send.settle()
    for copy in coming:
        copy.wait_recv()
    yield


def kernel(sizes, total, dosage, pheno, perm, snp_weight, out, *scratch):
    refs, position = [], 0
    for size in sizes:
        refs.append(scratch[position : position + size])
        position += size
    plain, pairs, (singles,) = refs
    pairs = [(pairs[i], pairs[i + 1]) for i in range(0, len(pairs), 2)]
    (
        coded, codes, placed, cols_in, early, turned, near_w, part, every,
        x_slots, acc, slots, chunk, gram, lower, start, first, second, partial, leaving,
        dose_here, perm_here,
    ) = plain
    at, send = Place(), Sender()
    barrier = pltpu.get_barrier_semaphore()
    greeted = [at.peer(*p) for p in at.peers]
    greeted += [{"x": at.across}, at.to_right, at.to_left]
    greeted += [at.far_cross, at.far, at.cross, at.near, at.sibling]
    for there in greeted:
        pl.semaphore_signal(barrier, inc=1, device_id=there, device_id_type=MESH)
    snps, own = dosage.shape
    mine = span(at.me, own)
    loads = [
        pltpu.make_async_copy(dosage, dose_here, singles.at[1]),
        pltpu.make_async_copy(perm, perm_here, singles.at[2]),
    ]
    for load in loads:
        load.start()
    for load in loads:
        load.wait()
    coded[:snps, mine] = dose_here[...].astype(F32).astype(BF16)
    source = perm_here[...]
    both = jnp.concatenate([lax.shift_right_logical(source, 8), source & 255], axis=0)
    coded[snps:, mine] = both.astype(F32).astype(BF16)
    pl.semaphore_wait(barrier, len(greeted))
    scores = score_steps(
        at, send, dosage, pheno, snp_weight, part, every,
        (coded, codes, placed, cols_in, early, turned, near_w, *pairs[:5], singles.at[0]),
    )
    moved = (
        x_slots, acc, slots, chunk, *pairs[5:11], singles.at[pl.ds(3, 2)], singles.at[pl.ds(5, 2)],
    )
    here, cross = (spread_chunk(at, send, total, part, gram, moved, k) for k in range(2))
    white = white_steps(
        at, send, pheno.shape[1], gram, every, out,
        (lower, start, first, second, partial, leaving, pairs[11]),
    )
    next(scores)
    next(here)
    next(scores)
    send.settle()
    next(here)
    next(scores)
    next(scores)
    next(cross)
    next(white)
    for _ in here:
        send.settle()
        next(cross)
    next(white)
    next(white)
    for _ in cross:
        send.settle()
        next(white)
    next(white)
    send.finish()


def shards(dosage, pheno, perm, snp_weight):
    snps, own = dosage.shape
    genes = pheno.shape[1]
    groups = lax.axis_size(SAMP)
    nulls = perm.shape[0]
    copies = nulls + 1
    rows = copies * snps
    cols = genes // groups
    samples = own * groups
    share = -(-rows // (16 * groups)) * 16
    tiles = 10
    most = max(n for _, n in CUTS) * 2 * TILE
    dma = pltpu.SemaphoreType.DMA
    vmem = pl.BlockSpec(memory_space=pltpu.VMEM)
    hbm = pl.BlockSpec(memory_space=pltpu.HBM)
    plain = [
        pltpu.VMEM((snps + 2 * nulls, samples), BF16),
        pltpu.VMEM((2 * nulls, samples), F32),
        pltpu.VMEM((LEAD + rows, samples), BF16),
        pltpu.VMEM((samples, cols), BF16),
        pltpu.VMEM((LEAD + rows, cols), F32),
        pltpu.VMEM((cols, rows - snps), BF16),
        pltpu.VMEM((rows - snps, 3 * cols), BF16),
        pltpu.VMEM((tiles * 2 * TILE, LANES), BF16),
        pltpu.VMEM((groups, share * groups, cols), BF16),
        pltpu.VMEM((2, 3, most // 4, LANES), BF16),
        pltpu.VMEM((2, most // 4, LANES), BF16),
        pltpu.VMEM((2, 16, most // 64, LANES), BF16),
        pltpu.VMEM((2, most // 64, LANES), BF16),
        pltpu.VMEM((groups, tiles * 2 * TILE, LANES), BF16),
        pltpu.VMEM((genes // TILE, TILE, 3 * TILE), BF16),
        *[pltpu.VMEM((genes, LANES), BF16)] * 3,
        pltpu.VMEM((genes, LANES), F32),
        pltpu.VMEM((3, share, cols), BF16),
        pltpu.VMEM(dosage.shape, jnp.int32),
        pltpu.VMEM(perm.shape, jnp.int32),
    ]
    each = len(CUTS)
    counts = [3, 5, 3, 3, 3, *[n * each for n in (3, 15, 15, 3, 8, 8)], 6]
    pairs = [dma((n,)) for n in counts for _ in range(2)]
    sizes = (len(plain), len(pairs), 1)
    white = pl.pallas_call(
        functools.partial(kernel, sizes, nulls * snps * lax.axis_size(SNP)),
        out_shape=jax.ShapeDtypeStruct((share * groups, cols), BF16),
        in_specs=[hbm, hbm, hbm, vmem],
        out_specs=vmem,
        scratch_shapes=[*plain, *pairs, dma((7,))],
        compiler_params=pltpu.CompilerParams(
            collective_id=0, has_side_effects=True, vmem_limit_bytes=60 << 20
        ),
        name="whitened_scores",
    )(dosage, pheno, perm, snp_weight[None, :])
    return white[:rows].reshape(copies, snps, cols)


def solution(mesh):
    finer = Mesh(mesh.devices.reshape(2, 2, 4, 8, 2), (*SAMP, *SNP))
    in_specs = (P(SNP, SAMP), P(SAMP, None), P(None, SAMP), P(SNP))
    return jax.shard_map(
        shards, mesh=finer, in_specs=in_specs, out_specs=P(None, SNP, SAMP), check_vma=False
    )
```
